256 devices in a mesh: seq: 16 (over z_lo, x), layer: 16 (over z_hi, y, core).
Axes of the slice: x: 4, y: 4, z: 8 (z_hi: 2, z_lo: 4; z = z_hi * 4 + z_lo), core: 2. Of those that a mesh axis runs over, the one named last changes fastest.
Arguments:
- train_inputs: bfloat16 [16, 2048, 4096], P('layer', 'seq'), may hold values from -6 to 6
- out_grads: bfloat16 [16, 2048, 14336], P('layer', 'seq'), may hold values from -6 to 6
- query_blocks: bfloat16 [16, 14336, 4096], P('layer', 'seq'), may hold values from -0.00018310547 to 0.00018310547
- basis_in: bfloat16 [16, 32, 128, 128], P('layer'), may hold values from -0.5 to 0.5
- basis_out: bfloat16 [16, 112, 128, 128], P('layer', 'seq'), may hold values from -0.5 to 0.5
- block_of: int32 [16, 16], P('layer'), may hold values from 0 to 15, each once within a row
Outputs:
- scores: float32 [2048], P('seq')
The draws below stay inside these ranges and needn't reach their ends.
Inputs may be any that keep to these rules, and one draw needn't show every extreme that they name: Each row of block_of names every eigenbasis block of its layer once.
All inputs are finite; a program needn't handle non-finite values.
Results may differ from the reference program's by a relative error of at most 0.0055.
Values may be sent and summed in bfloat16 or wider, within the bound.
A program may use at most 128 MiB of HBM per device.

```python
import jax
import jax.numpy as jnp
from jax import lax

D_IN = 4096
D_OUT = 14336
RB = 128
TOKENS = 2048
LAYERS = 16
NBLK = 16


def steps_of(own_key, shape, cuts, least, high):
    level = 1.0
    for dim, blocks in cuts:
        heights = jax.random.uniform(jax.random.fold_in(jax.random.fold_in(own_key, 6), dim), (blocks,), jnp.float32, least / len(cuts), high / len(cuts))
        level = level * jnp.repeat(jnp.exp(heights), shape[dim] // blocks).reshape((-1,) + (1,) * (len(shape) - 1 - dim))
    return level


def gaussian(own_key, shape, spread, reach, pieces=(), dtype=jnp.bfloat16):
    entries = spread * jax.random.normal(own_key, shape, jnp.float32)
    if pieces:
        entries = entries * steps_of(own_key, shape, pieces, -0.22, 0.18)
    return jnp.clip(entries, -reach, reach).astype(dtype)


def setup_inputs(seed: int = 0) -> dict:
    key_of = jax.random.split(jax.random.key(seed), 7)
    return {
        "train_inputs": gaussian(key_of[0], (LAYERS, TOKENS, D_IN), 1.0, 6.0, ((0, 16), (1, 16))),
        "out_grads": gaussian(key_of[1], (LAYERS, TOKENS, D_OUT), 1.0, 6.0, ((0, 16), (1, 16))),
        "query_blocks": gaussian(key_of[2], (LAYERS, D_OUT, D_IN), (LAYERS * D_OUT * D_IN) ** -0.5, 0.00018310547, ((0, 16), (1, 16))),
        "basis_in": gaussian(key_of[3], (LAYERS, D_IN // RB, RB, RB), RB ** -0.5, 0.5, ((0, 16),)),
        "basis_out": gaussian(key_of[4], (LAYERS, D_OUT // RB, RB, RB), RB ** -0.5, 0.5, ((0, 16), (1, 16))),
        "block_of": jax.vmap(lambda own: jax.random.permutation(own, NBLK))(jax.random.split(key_of[5], LAYERS)).reshape((LAYERS, NBLK)).astype(jnp.int32),
    }


def turn_rows(rows, basis):
    count = rows.shape[0]
    groups = rows.reshape(count, basis.shape[0], basis.shape[1]).astype(jnp.float32)
    turned = jnp.einsum('tnr,nrs->tns', groups, basis.astype(jnp.float32))
    return turned.reshape(count, -1).astype(jnp.bfloat16)


def reference(train_inputs, out_grads, query_blocks, basis_in, basis_out, block_of):
    def one_layer(total, items):
        acts, grads, query, rot_in, rot_out, owners = items
        count = acts.shape[0]
        rotated = turn_rows(acts, rot_in)
        picked = jnp.take(grads.reshape(count, owners.shape[0], -1), owners.astype(jnp.int32), axis=1)
        turned = turn_rows(picked.reshape(count, -1), rot_out)
        projected = lax.dot_general(rotated, query, (((1,), (1,)), ((), ())), preferred_element_type=jnp.float32)
        return total + jnp.sum(projected * turned.astype(jnp.float32), axis=1), None

    start_total = jnp.zeros((train_inputs.shape[1],), jnp.float32)
    total, _ = lax.scan(one_layer, start_total, (train_inputs, out_grads, query_blocks, basis_in, basis_out, block_of))
    return total
```

```python
import functools

import jax
import jax.numpy as jnp
from jax import lax
from jax.experimental import pallas as pl
from jax.experimental.pallas import tpu as pltpu
from jax.sharding import PartitionSpec as P

MESH = pl.DeviceIdType.MESH


def turn_rows(rows, basis):
    count = rows.shape[0]
    groups = rows.reshape(count, basis.shape[0], basis.shape[1])
    turned = jnp.einsum("tnr,nrs->tns", groups, basis, preferred_element_type=jnp.float32)
    return turned.reshape(count, -1).astype(jnp.bfloat16)


def reduce_kernel(ns, nl, part_ref, out_ref, slots1, mine, slots2, ssem1, rsem1, ssem2, rsem2):
    ms = lax.axis_index("seq")
    ml = lax.axis_index("layer")
    barrier = pltpu.get_barrier_semaphore()
    for d in range(1, ns):
        pl.semaphore_signal(barrier, inc=1, device_id=(lax.rem(ms + d, ns), ml), device_id_type=MESH)
    for d in range(1, nl):
        pl.semaphore_signal(barrier, inc=1, device_id=(ms, lax.rem(ml + d, nl)), device_id_type=MESH)
    pl.semaphore_wait(barrier, (ns - 1) + (nl - 1))

    sends = []
    for d in range(1, ns):
        j = lax.rem(ms + d, ns)
        c = pltpu.make_async_remote_copy(
            src_ref=part_ref.at[j], dst_ref=slots1.at[ms], send_sem=ssem1.at[j], recv_sem=rsem1.at[ms],
            device_id=(j, ml), device_id_type=MESH)
        c.start()
        sends.append(c)
    slots1[ms] = part_ref[ms]
    for d in range(1, ns):
        i = lax.rem(ms + ns - d, ns)
        pltpu.make_async_remote_copy(
            src_ref=part_ref.at[i], dst_ref=slots1.at[i], send_sem=ssem1.at[i], recv_sem=rsem1.at[i],
            device_id=(i, ml), device_id_type=MESH).wait_recv()
    for c in sends:
        c.wait_send()
    acc = slots1[0]
    for i in range(1, ns):
        acc = acc + slots1[i]
    mine[...] = acc

    sends = []
    for d in range(1, nl):
        j = lax.rem(ml + d, nl)
        c = pltpu.make_async_remote_copy(
            src_ref=mine, dst_ref=slots2.at[ml], send_sem=ssem2.at[j], recv_sem=rsem2.at[ml],
            device_id=(ms, j), device_id_type=MESH)
        c.start()
        sends.append(c)
    slots2[ml] = acc
    for d in range(1, nl):
        i = lax.rem(ml + nl - d, nl)
        pltpu.make_async_remote_copy(
            src_ref=mine, dst_ref=slots2.at[i], send_sem=ssem2.at[i], recv_sem=rsem2.at[i],
            device_id=(ms, i), device_id_type=MESH).wait_recv()
    for c in sends:
        c.wait_send()
    tot = slots2[0]
    for i in range(1, nl):
        tot = tot + slots2[i]
    out_ref[...] = tot


def reduce_scores(partial, ns, nl):
    w = partial.shape[0] // ns
    part = partial.reshape(ns, 1, w)
    out = pl.pallas_call(
        functools.partial(reduce_kernel, ns, nl),
        out_shape=jax.ShapeDtypeStruct((1, w), jnp.float32),
        in_specs=[pl.BlockSpec(memory_space=pltpu.VMEM)],
        out_specs=pl.BlockSpec(memory_space=pltpu.VMEM),
        scratch_shapes=[
            pltpu.VMEM((ns, 1, w), jnp.float32),
            pltpu.VMEM((1, w), jnp.float32),
            pltpu.VMEM((nl, 1, w), jnp.float32),
            pltpu.SemaphoreType.DMA((ns,)),
            pltpu.SemaphoreType.DMA((ns,)),
            pltpu.SemaphoreType.DMA((nl,)),
            pltpu.SemaphoreType.DMA((nl,)),
        ],
        compiler_params=pltpu.CompilerParams(collective_id=0, has_side_effects=True),
    )(part)
    return out.reshape(w)


def body(ns, nl, train_inputs, out_grads, query_blocks, basis_in, basis_out, block_of):
    acts = train_inputs[0]
    grads = out_grads[0]
    query = query_blocks[0]
    owners = block_of[0]
    count = acts.shape[0]
    rotated = turn_rows(acts, basis_in[0])
    outgoing = jnp.take(grads.reshape(count, owners.shape[0], -1), owners, axis=1)
    arrived = lax.all_to_all(outgoing, "seq", split_axis=1, concat_axis=0, tiled=True)
    turned = turn_rows(arrived.reshape(arrived.shape[0], -1), basis_out[0])
    partial_scores = jnp.sum(
        lax.dot_general(
            lax.all_gather(rotated, "seq", axis=0, tiled=True),
            query,
            (((1,), (1,)), ((), ())),
            preferred_element_type=jnp.float32,
        )
        * turned.astype(jnp.float32),
        axis=1,
    )
    return reduce_scores(partial_scores, ns, nl)


def solution(mesh):
    ns, nl = mesh.shape["seq"], mesh.shape["layer"]
    placed = (
        P("layer", "seq", None),
        P("layer", "seq", None),
        P("layer", "seq", None),
        P("layer", None, None, None),
        P("layer", "seq", None, None),
        P("layer", None),
    )
    return jax.shard_map(functools.partial(body, ns, nl), mesh=mesh, in_specs=placed, out_specs=P("seq"), check_vma=False)
```

```python
import functools

import jax
import jax.numpy as jnp
from jax import lax
from jax.experimental import pallas as pl
from jax.experimental.pallas import tpu as pltpu
from jax.sharding import PartitionSpec as P

MESH = pl.DeviceIdType.MESH


def turn_rows(rows, basis):
    count = rows.shape[0]
    groups = rows.reshape(count, basis.shape[0], basis.shape[1])
    turned = jnp.einsum("tnr,nrs->tns", groups, basis, preferred_element_type=jnp.float32)
    return turned.reshape(count, -1).astype(jnp.bfloat16)


def reduce_kernel(ns, nl, part_ref, out_ref, slots1, mine, slots2, ssem1, rsem1, ssem2, rsem2):
    ms = lax.axis_index("seq")
    ml = lax.axis_index("layer")
    barrier = pltpu.get_barrier_semaphore()
    for d in range(1, ns):
        pl.semaphore_signal(barrier, inc=1, device_id=(lax.rem(ms + d, ns), ml), device_id_type=MESH)
    for d in range(1, nl):
        pl.semaphore_signal(barrier, inc=1, device_id=(ms, lax.rem(ml + d, nl)), device_id_type=MESH)
    pl.semaphore_wait(barrier, (ns - 1) + (nl - 1))

    sends = []
    for d in range(1, ns):
        j = lax.rem(ms + d, ns)
        c = pltpu.make_async_remote_copy(
            src_ref=part_ref.at[j], dst_ref=slots1.at[ms], send_sem=ssem1.at[j], recv_sem=rsem1.at[ms],
            device_id=(j, ml), device_id_type=MESH)
        c.start()
        sends.append(c)
    slots1[ms] = part_ref[ms]
    for d in range(1, ns):
        i = lax.rem(ms + ns - d, ns)
        pltpu.make_async_remote_copy(
            src_ref=part_ref.at[i], dst_ref=slots1.at[i], send_sem=ssem1.at[i], recv_sem=rsem1.at[i],
            device_id=(i, ml), device_id_type=MESH).wait_recv()
    for c in sends:
        c.wait_send()
    acc = slots1[0]
    for i in range(1, ns):
        acc = acc + slots1[i]
    mine[...] = acc

    sends = []
    for d in range(1, nl):
        j = lax.rem(ml + d, nl)
        c = pltpu.make_async_remote_copy(
            src_ref=mine, dst_ref=slots2.at[ml], send_sem=ssem2.at[j], recv_sem=rsem2.at[ml],
            device_id=(ms, j), device_id_type=MESH)
        c.start()
        sends.append(c)
    slots2[ml] = acc
    for d in range(1, nl):
        i = lax.rem(ml + nl - d, nl)
        pltpu.make_async_remote_copy(
            src_ref=mine, dst_ref=slots2.at[i], send_sem=ssem2.at[i], recv_sem=rsem2.at[i],
            device_id=(ms, i), device_id_type=MESH).wait_recv()
    for c in sends:
        c.wait_send()
    tot = slots2[0]
    for i in range(1, nl):
        tot = tot + slots2[i]
    out_ref[...] = tot


def comm_kernel(nx, nz, r1, x_ref, g_ref, xo_ref, go_ref, ssem, rsem, gssem, grsem, lsem):
    ns = nx * nz
    t = x_ref.shape[0]
    s = lax.axis_index("seq")
    lay = lax.axis_index("layer")
    zl = s // nx
    xx = lax.rem(s, nx)
    parts = (pl.ds(0, r1), pl.ds(r1, t - r1))

    def at(dz, dx):
        return lax.rem(zl + dz, nz) * nx + lax.rem(xx + dx, nx)

    barrier = pltpu.get_barrier_semaphore()
    for d in range(1, ns):
        pl.semaphore_signal(barrier, inc=1, device_id=(lax.rem(s + d, ns), lay), device_id_type=MESH)
    pl.semaphore_wait(barrier, ns - 1)

    own_x = pltpu.make_async_copy(x_ref, xo_ref.at[s], lsem.at[0])
    own_g = pltpu.make_async_copy(g_ref.at[s], go_ref.at[s], lsem.at[1])
    own_x.start()
    own_g.start()

    sends = []

    def send(src, slot, part, dst):
        c = pltpu.make_async_remote_copy(
            src_ref=src, dst_ref=xo_ref.at[slot, parts[part]], send_sem=ssem.at[len(sends)],
            recv_sem=rsem.at[slot * 2 + part], device_id=(dst, lay), device_id_type=MESH)
        c.start()
        sends.append(c)

    def recv(slot, part):
        pltpu.make_async_remote_copy(
            src_ref=x_ref.at[parts[part]], dst_ref=xo_ref.at[slot, parts[part]], send_sem=ssem.at[0],
            recv_sem=rsem.at[slot * 2 + part], device_id=(slot, lay), device_id_type=MESH).wait_recv()

    for dx in range(1, nx):
        send(x_ref.at[parts[0]], s, 0, at(0, dx))
    for dz in range(1, nz):
        send(x_ref.at[parts[1]], s, 1, at(dz, 0))
    for dz in range(1, nz):
        send(x_ref.at[parts[0]], s, 0, at(dz, 0))
    for dx in range(1, nx):
        send(x_ref.at[parts[1]], s, 1, at(0, dx))
    gsends = []
    for d in range(1, ns):
        j = lax.rem(s + d, ns)
        c = pltpu.make_async_remote_copy(
            src_ref=g_ref.at[j], dst_ref=go_ref.at[s], send_sem=gssem.at[d - 1],
            recv_sem=grsem.at[s], device_id=(j, lay), device_id_type=MESH)
        c.start()
        gsends.append(c)
    for dx in range(1, nx):
        q = at(0, dx)
        recv(q, 0)
        for dz in range(1, nz):
            send(xo_ref.at[q, parts[0]], q, 0, at(dz, 0))
    for dz in range(1, nz):
        q = at(dz, 0)
        recv(q, 1)
        for dx in range(1, nx):
            send(xo_ref.at[q, parts[1]], q, 1, at(0, dx))
    for dz in range(1, nz):
        for dx in range(nx):
            recv(at(dz, dx), 0)
    for dx in range(1, nx):
        for dz in range(nz):
            recv(at(dz, dx), 1)
    for d in range(1, ns):
        i = lax.rem(s + ns - d, ns)
        pltpu.make_async_remote_copy(
            src_ref=g_ref.at[i], dst_ref=go_ref.at[i], send_sem=gssem.at[d - 1],
            recv_sem=grsem.at[i], device_id=(i, lay), device_id_type=MESH).wait_recv()
    for c in sends + gsends:
        c.wait_send()
    own_x.wait()
    own_g.wait()


def exchange(rotated, outgoing, ns):
    nx = 4 if ns % 4 == 0 else 1
    nz = ns // nx
    t, dim = rotated.shape
    w = outgoing.shape[-1]
    r1 = (t * 3 // 8) // 16 * 16
    n_sends = 2 * ((nx - 1) + (nz - 1)) + (nx - 1) * (nz - 1) * 2
    return pl.pallas_call(
        functools.partial(comm_kernel, nx, nz, r1),
        out_shape=(jax.ShapeDtypeStruct((ns, t, dim), rotated.dtype), jax.ShapeDtypeStruct((ns, t, w), outgoing.dtype)),
        in_specs=[pl.BlockSpec(memory_space=pl.ANY)] * 2,
        out_specs=(pl.BlockSpec(memory_space=pl.ANY), pl.BlockSpec(memory_space=pl.ANY)),
        scratch_shapes=[
            pltpu.SemaphoreType.DMA((n_sends,)),
            pltpu.SemaphoreType.DMA((2 * ns,)),
            pltpu.SemaphoreType.DMA((ns - 1,)),
            pltpu.SemaphoreType.DMA((ns,)),
            pltpu.SemaphoreType.DMA((2,)),
        ],
        compiler_params=pltpu.CompilerParams(collective_id=1, has_side_effects=True),
    )(rotated, outgoing)


def reduce_scores(partial, ns, nl):
    w = partial.shape[0] // ns
    part = partial.reshape(ns, 1, w)
    out = pl.pallas_call(
        functools.partial(reduce_kernel, ns, nl),
        out_shape=jax.ShapeDtypeStruct((1, w), jnp.float32),
        in_specs=[pl.BlockSpec(memory_space=pltpu.VMEM)],
        out_specs=pl.BlockSpec(memory_space=pltpu.VMEM),
        scratch_shapes=[
            pltpu.VMEM((ns, 1, w), jnp.float32),
            pltpu.VMEM((1, w), jnp.float32),
            pltpu.VMEM((nl, 1, w), jnp.float32),
            pltpu.SemaphoreType.DMA((ns,)),
            pltpu.SemaphoreType.DMA((ns,)),
            pltpu.SemaphoreType.DMA((nl,)),
            pltpu.SemaphoreType.DMA((nl,)),
        ],
        compiler_params=pltpu.CompilerParams(collective_id=0, has_side_effects=True),
    )(part)
    return out.reshape(w)


def body(ns, nl, train_inputs, out_grads, query_blocks, basis_in, basis_out, block_of):
    acts = train_inputs[0]
    grads = out_grads[0]
    query = query_blocks[0]
    owners = block_of[0]
    count = acts.shape[0]
    rotated = turn_rows(acts, basis_in[0])
    outgoing = jnp.take(grads.reshape(count, owners.shape[0], -1), owners, axis=1).transpose(1, 0, 2)
    gathered, arrived = exchange(rotated, outgoing, ns)
    turned = turn_rows(arrived.reshape(ns * count, -1), basis_out[0])
    partial_scores = jnp.sum(
        lax.dot_general(
            gathered.reshape(ns * count, -1),
            query,
            (((1,), (1,)), ((), ())),
            preferred_element_type=jnp.float32,
        )
        * turned.astype(jnp.float32),
        axis=1,
    )
    return reduce_scores(partial_scores, ns, nl)


def solution(mesh):
    ns, nl = mesh.shape["seq"], mesh.shape["layer"]
    placed = (
        P("layer", "seq", None),
        P("layer", "seq", None),
        P("layer", "seq", None),
        P("layer", None, None, None),
        P("layer", "seq", None, None),
        P("layer", None),
    )
    return jax.shard_map(functools.partial(body, ns, nl), mesh=mesh, in_specs=placed, out_specs=P("seq"), check_vma=False)
```

```python
import functools

import jax
import jax.numpy as jnp
from jax import lax
from jax.experimental import pallas as pl
from jax.experimental.pallas import tpu as pltpu
from jax.sharding import PartitionSpec as P

MESH = pl.DeviceIdType.MESH


def turn_rows(rows, basis):
    count = rows.shape[0]
    groups = rows.reshape(count, basis.shape[0], basis.shape[1])
    turned = jnp.einsum("tnr,nrs->tns", groups, basis, preferred_element_type=jnp.float32)
    return turned.reshape(count, -1).astype(jnp.bfloat16)


def reduce_kernel(ns, nl, part_ref, out_ref, slots1, mine, slots2, ssem1, rsem1, ssem2, rsem2):
    ms = lax.axis_index("seq")
    ml = lax.axis_index("layer")
    barrier = pltpu.get_barrier_semaphore()
    for d in range(1, ns):
        pl.semaphore_signal(barrier, inc=1, device_id=(lax.rem(ms + d, ns), ml), device_id_type=MESH)
    for d in range(1, nl):
        pl.semaphore_signal(barrier, inc=1, device_id=(ms, lax.rem(ml + d, nl)), device_id_type=MESH)
    pl.semaphore_wait(barrier, (ns - 1) + (nl - 1))

    sends = []
    for d in range(1, ns):
        j = lax.rem(ms + d, ns)
        c = pltpu.make_async_remote_copy(
            src_ref=part_ref.at[j], dst_ref=slots1.at[ms], send_sem=ssem1.at[j], recv_sem=rsem1.at[ms],
            device_id=(j, ml), device_id_type=MESH)
        c.start()
        sends.append(c)
    slots1[ms] = part_ref[ms]
    for d in range(1, ns):
        i = lax.rem(ms + ns - d, ns)
        pltpu.make_async_remote_copy(
            src_ref=part_ref.at[i], dst_ref=slots1.at[i], send_sem=ssem1.at[i], recv_sem=rsem1.at[i],
            device_id=(i, ml), device_id_type=MESH).wait_recv()
    for c in sends:
        c.wait_send()
    acc = slots1[0]
    for i in range(1, ns):
        acc = acc + slots1[i]
    mine[...] = acc

    sends = []
    for d in range(1, nl):
        j = lax.rem(ml + d, nl)
        c = pltpu.make_async_remote_copy(
            src_ref=mine, dst_ref=slots2.at[ml], send_sem=ssem2.at[j], recv_sem=rsem2.at[ml],
            device_id=(ms, j), device_id_type=MESH)
        c.start()
        sends.append(c)
    slots2[ml] = acc
    for d in range(1, nl):
        i = lax.rem(ml + nl - d, nl)
        pltpu.make_async_remote_copy(
            src_ref=mine, dst_ref=slots2.at[i], send_sem=ssem2.at[i], recv_sem=rsem2.at[i],
            device_id=(ms, i), device_id_type=MESH).wait_recv()
    for c in sends:
        c.wait_send()
    tot = slots2[0]
    for i in range(1, nl):
        tot = tot + slots2[i]
    out_ref[...] = tot


def comm_kernel(nx, nz, r1, x_ref, g_ref, xo_ref, go_ref, ssem, rsem, gssem, grsem, lsem):
    ns = nx * nz
    t = x_ref.shape[0]
    s = lax.axis_index("seq")
    lay = lax.axis_index("layer")
    zl = s // nx
    xx = lax.rem(s, nx)
    parts = (pl.ds(0, r1), pl.ds(r1, t - r1))

    def at(dz, dx):
        return lax.rem(zl + dz, nz) * nx + lax.rem(xx + dx, nx)

    barrier = pltpu.get_barrier_semaphore()
    for d in range(1, ns):
        pl.semaphore_signal(barrier, inc=1, device_id=(lax.rem(s + d, ns), lay), device_id_type=MESH)
    pl.semaphore_wait(barrier, ns - 1)

    own_x = pltpu.make_async_copy(x_ref, xo_ref.at[s], lsem.at[0])
    own_g = pltpu.make_async_copy(g_ref.at[s], go_ref.at[s], lsem.at[1])
    own_x.start()
    own_g.start()

    sends = []

    def send(src, slot, part, dst):
        c = pltpu.make_async_remote_copy(
            src_ref=src, dst_ref=xo_ref.at[slot, parts[part]], send_sem=ssem.at[len(sends)],
            recv_sem=rsem.at[slot * 2 + part], device_id=(dst, lay), device_id_type=MESH)
        c.start()
        sends.append(c)

    def recv(slot, part):
        pltpu.make_async_remote_copy(
            src_ref=x_ref.at[parts[part]], dst_ref=xo_ref.at[slot, parts[part]], send_sem=ssem.at[0],
            recv_sem=rsem.at[slot * 2 + part], device_id=(slot, lay), device_id_type=MESH).wait_recv()

    for dx in range(1, nx):
        send(x_ref.at[parts[0]], s, 0, at(0, dx))
    for dz in range(1, nz):
        send(x_ref.at[parts[1]], s, 1, at(dz, 0))
    for dz in range(1, nz):
        send(x_ref.at[parts[0]], s, 0, at(dz, 0))
    for dx in range(1, nx):
        send(x_ref.at[parts[1]], s, 1, at(0, dx))
    gsends = []
    for d in range(1, ns):
        j = lax.rem(s + d, ns)
        c = pltpu.make_async_remote_copy(
            src_ref=g_ref.at[j], dst_ref=go_ref.at[s], send_sem=gssem.at[d - 1],
            recv_sem=grsem.at[s], device_id=(j, lay), device_id_type=MESH)
        c.start()
        gsends.append(c)
    for dx in range(1, nx):
        q = at(0, dx)
        recv(q, 0)
        for dz in range(1, nz):
            send(xo_ref.at[q, parts[0]], q, 0, at(dz, 0))
    for dz in range(1, nz):
        q = at(dz, 0)
        recv(q, 1)
        for dx in range(1, nx):
            send(xo_ref.at[q, parts[1]], q, 1, at(0, dx))
    for dz in range(1, nz):
        for dx in range(nx):
            recv(at(dz, dx), 0)
    for dx in range(1, nx):
        for dz in range(nz):
            recv(at(dz, dx), 1)
    for d in range(1, ns):
        i = lax.rem(s + ns - d, ns)
        pltpu.make_async_remote_copy(
            src_ref=g_ref.at[i], dst_ref=go_ref.at[i], send_sem=gssem.at[d - 1],
            recv_sem=grsem.at[i], device_id=(i, lay), device_id_type=MESH).wait_recv()
    for c in sends + gsends:
        c.wait_send()
    own_x.wait()
    own_g.wait()


def exchange(rotated, outgoing, ns):
    nx = 4 if ns % 4 == 0 else 1
    nz = ns // nx
    t, dim = rotated.shape
    w = outgoing.shape[-1]
    r1 = (t * 3 // 8) // 16 * 16
    n_sends = 2 * ((nx - 1) + (nz - 1)) + (nx - 1) * (nz - 1) * 2
    return pl.pallas_call(
        functools.partial(comm_kernel, nx, nz, r1),
        out_shape=(jax.ShapeDtypeStruct((ns, t, dim), rotated.dtype), jax.ShapeDtypeStruct((ns, t, w), outgoing.dtype)),
        in_specs=[pl.BlockSpec(memory_space=pl.ANY)] * 2,
        out_specs=(pl.BlockSpec(memory_space=pl.ANY), pl.BlockSpec(memory_space=pl.ANY)),
        scratch_shapes=[
            pltpu.SemaphoreType.DMA((n_sends,)),
            pltpu.SemaphoreType.DMA((2 * ns,)),
            pltpu.SemaphoreType.DMA((ns - 1,)),
            pltpu.SemaphoreType.DMA((ns,)),
            pltpu.SemaphoreType.DMA((2,)),
        ],
        compiler_params=pltpu.CompilerParams(collective_id=1, has_side_effects=True),
    )(rotated, outgoing)


def reduce_scores(partial, ns, nl):
    w = partial.shape[0] // ns
    part = partial.reshape(ns, 1, w)
    out = pl.pallas_call(
        functools.partial(reduce_kernel, ns, nl),
        out_shape=jax.ShapeDtypeStruct((1, w), jnp.float32),
        in_specs=[pl.BlockSpec(memory_space=pltpu.VMEM)],
        out_specs=pl.BlockSpec(memory_space=pltpu.VMEM),
        scratch_shapes=[
            pltpu.VMEM((ns, 1, w), jnp.float32),
            pltpu.VMEM((1, w), jnp.float32),
            pltpu.VMEM((nl, 1, w), jnp.float32),
            pltpu.SemaphoreType.DMA((ns,)),
            pltpu.SemaphoreType.DMA((ns,)),
            pltpu.SemaphoreType.DMA((nl,)),
            pltpu.SemaphoreType.DMA((nl,)),
        ],
        compiler_params=pltpu.CompilerParams(collective_id=0, has_side_effects=True),
    )(part)
    return out.reshape(w)


def body(ns, nl, train_inputs, out_grads, query_blocks, basis_in, basis_out, block_of):
    acts = train_inputs[0]
    grads = out_grads[0]
    query = query_blocks[0]
    owners = block_of[0]
    count = acts.shape[0]
    rotated = turn_rows(acts, basis_in[0])
    width = grads.shape[1] // owners.shape[0]
    outgoing = jnp.stack([lax.dynamic_slice_in_dim(grads, owners[k] * width, width, axis=1) for k in range(owners.shape[0])])
    gathered, arrived = exchange(rotated, outgoing, ns)
    arrived = arrived.reshape(ns * count, width)
    rb = basis_out.shape[-1]
    turned = jnp.concatenate(
        [jnp.dot(arrived[:, e * rb:(e + 1) * rb], basis_out[0, e], preferred_element_type=jnp.float32) for e in range(basis_out.shape[1])],
        axis=1).astype(jnp.bfloat16)
    partial_scores = jnp.sum(
        lax.dot_general(
            gathered.reshape(ns * count, -1),
            query,
            (((1,), (1,)), ((), ())),
            preferred_element_type=jnp.float32,
        )
        * turned.astype(jnp.float32),
        axis=1,
    )
    return reduce_scores(partial_scores, ns, nl)


def solution(mesh):
    ns, nl = mesh.shape["seq"], mesh.shape["layer"]
    placed = (
        P("layer", "seq", None),
        P("layer", "seq", None),
        P("layer", "seq", None),
        P("layer", None, None, None),
        P("layer", "seq", None, None),
        P("layer", None),
    )
    return jax.shard_map(functools.partial(body, ns, nl), mesh=mesh, in_specs=placed, out_specs=P("seq"), check_vma=False)
```

```python
import functools

import jax
import jax.numpy as jnp
from jax import lax
from jax.experimental import pallas as pl
from jax.experimental.pallas import tpu as pltpu
from jax.sharding import PartitionSpec as P

MESH = pl.DeviceIdType.MESH


def turn_rows(rows, basis):
    count = rows.shape[0]
    groups = rows.reshape(count, basis.shape[0], basis.shape[1])
    turned = jnp.einsum("tnr,nrs->tns", groups, basis, preferred_element_type=jnp.float32)
    return turned.reshape(count, -1).astype(jnp.bfloat16)


def reduce_kernel(ns, nl, part_ref, out_ref, slots1, mine, slots2, ssem1, rsem1, ssem2, rsem2):
    ms = lax.axis_index("seq")
    ml = lax.axis_index("layer")
    barrier = pltpu.get_barrier_semaphore()
    for d in range(1, ns):
        pl.semaphore_signal(barrier, inc=1, device_id=(lax.rem(ms + d, ns), ml), device_id_type=MESH)
    for d in range(1, nl):
        pl.semaphore_signal(barrier, inc=1, device_id=(ms, lax.rem(ml + d, nl)), device_id_type=MESH)
    pl.semaphore_wait(barrier, (ns - 1) + (nl - 1))

    sends = []
    for d in range(1, ns):
        j = lax.rem(ms + d, ns)
        c = pltpu.make_async_remote_copy(
            src_ref=part_ref.at[j], dst_ref=slots1.at[ms], send_sem=ssem1.at[j], recv_sem=rsem1.at[ms],
            device_id=(j, ml), device_id_type=MESH)
        c.start()
        sends.append(c)
    slots1[ms] = part_ref[ms]
    for d in range(1, ns):
        i = lax.rem(ms + ns - d, ns)
        pltpu.make_async_remote_copy(
            src_ref=part_ref.at[i], dst_ref=slots1.at[i], send_sem=ssem1.at[i], recv_sem=rsem1.at[i],
            device_id=(i, ml), device_id_type=MESH).wait_recv()
    for c in sends:
        c.wait_send()
    acc = slots1[0]
    for i in range(1, ns):
        acc = acc + slots1[i]
    mine[...] = acc

    sends = []
    for d in range(1, nl):
        j = lax.rem(ml + d, nl)
        c = pltpu.make_async_remote_copy(
            src_ref=mine, dst_ref=slots2.at[ml], send_sem=ssem2.at[j], recv_sem=rsem2.at[ml],
            device_id=(ms, j), device_id_type=MESH)
        c.start()
        sends.append(c)
    slots2[ml] = acc
    for d in range(1, nl):
        i = lax.rem(ml + nl - d, nl)
        pltpu.make_async_remote_copy(
            src_ref=mine, dst_ref=slots2.at[i], send_sem=ssem2.at[i], recv_sem=rsem2.at[i],
            device_id=(ms, i), device_id_type=MESH).wait_recv()
    for c in sends:
        c.wait_send()
    tot = slots2[0]
    for i in range(1, nl):
        tot = tot + slots2[i]
    out_ref[...] = tot


def comm_kernel(nx, nz, r1, x_ref, g_ref, xo_ref, go_ref, ssem, rsem, gssem, grsem, lsem):
    ns = nx * nz
    t = x_ref.shape[0]
    s = lax.axis_index("seq")
    lay = lax.axis_index("layer")
    zl = s // nx
    xx = lax.rem(s, nx)
    ha, hb = r1 // 2, (t - r1) // 2
    halves = ((pl.ds(0, ha), pl.ds(ha, ha)), (pl.ds(r1, hb), pl.ds(r1 + hb, hb)))
    whole = (pl.ds(0, r1), pl.ds(r1, t - r1))

    def at(dz, dx):
        return lax.rem(zl + dz + nz, nz) * nx + lax.rem(xx + dx + nx, nx)

    barrier = pltpu.get_barrier_semaphore()
    for d in range(1, ns):
        pl.semaphore_signal(barrier, inc=1, device_id=(lax.rem(s + d, ns), lay), device_id_type=MESH)
    pl.semaphore_wait(barrier, ns - 1)

    own_x = pltpu.make_async_copy(x_ref, xo_ref.at[s], lsem.at[0])
    own_g = pltpu.make_async_copy(g_ref.at[s], go_ref.at[s], lsem.at[1])
    own_x.start()
    own_g.start()

    sends = []

    def rows(part, half):
        return whole[part] if half is None else halves[part][half]

    def sem(slot, part, half):
        return rsem.at[slot * 4 + part * 2 + (0 if half is None else half)]

    def send(dz, dx, part, half, to):
        slot = at(dz, dx)
        rr = rows(part, half)
        src = x_ref.at[rr] if (dz, dx) == (0, 0) else xo_ref.at[slot, rr]
        c = pltpu.make_async_remote_copy(
            src_ref=src, dst_ref=xo_ref.at[slot, rr], send_sem=ssem.at[len(sends)],
            recv_sem=sem(slot, part, half), device_id=(to, lay), device_id_type=MESH)
        c.start()
        sends.append(c)

    def recv(dz, dx, part, half):
        slot = at(dz, dx)
        rr = rows(part, half)
        pltpu.make_async_remote_copy(
            src_ref=x_ref.at[rr], dst_ref=xo_ref.at[slot, rr], send_sem=ssem.at[0],
            recv_sem=sem(slot, part, half), device_id=(slot, lay), device_id_type=MESH).wait_recv()

    right, left = at(0, 1), at(0, -1)
    zpeers = [at(dz, 0) for dz in range(1, nz)]
    for h in range(2):
        send(0, 0, 0, h, right)
        send(0, 0, 0, h, left)
    for zp in zpeers:
        send(0, 0, 0, None, zp)
        send(0, 0, 1, None, zp)
    for h in range(2):
        send(0, 0, 1, h, right)
        send(0, 0, 1, h, left)
    gsends = []
    for d in range(1, ns):
        j = lax.rem(s + d, ns)
        c = pltpu.make_async_remote_copy(
            src_ref=g_ref.at[j], dst_ref=go_ref.at[s], send_sem=gssem.at[d - 1],
            recv_sem=grsem.at[s], device_id=(j, lay), device_id_type=MESH)
        c.start()
        gsends.append(c)
    recv(0, -1, 0, 0)
    send(0, -1, 0, 0, right)
    recv(0, 1, 0, 1)
    send(0, 1, 0, 1, left)
    recv(0, -1, 0, 1)
    recv(0, 1, 0, 0)
    for dx in (-1, 1):
        for zp in zpeers:
            send(0, dx, 0, None, zp)
    recv(0, 2, 0, 0)
    recv(0, 2, 0, 1)
    for zp in zpeers:
        send(0, 2, 0, None, zp)
    for dz in range(1, nz):
        recv(dz, 0, 1, None)
        for h in range(2):
            send(dz, 0, 1, h, right)
            send(dz, 0, 1, h, left)
    for dz in range(nz):
        recv(dz, -1, 1, 0)
        send(dz, -1, 1, 0, right)
        recv(dz, 1, 1, 1)
        send(dz, 1, 1, 1, left)
    for dz in range(1, nz):
        for dx in range(nx):
            recv(dz, dx, 0, None)
    for dz in range(nz):
        recv(dz, -1, 1, 1)
        recv(dz, 1, 1, 0)
        recv(dz, 2, 1, 0)
        recv(dz, 2, 1, 1)
    for d in range(1, ns):
        i = lax.rem(s + ns - d, ns)
        pltpu.make_async_remote_copy(
            src_ref=g_ref.at[i], dst_ref=go_ref.at[i], send_sem=gssem.at[d - 1],
            recv_sem=grsem.at[i], device_id=(i, lay), device_id_type=MESH).wait_recv()
    for c in sends + gsends:
        c.wait_send()
    own_x.wait()
    own_g.wait()


def exchange(rotated, outgoing, ns):
    nx = 4
    nz = ns // nx
    t, dim = rotated.shape
    w = outgoing.shape[-1]
    r1 = t // 8
    n_sends = 64
    return pl.pallas_call(
        functools.partial(comm_kernel, nx, nz, r1),
        out_shape=(jax.ShapeDtypeStruct((ns, t, dim), rotated.dtype), jax.ShapeDtypeStruct((ns, t, w), outgoing.dtype)),
        in_specs=[pl.BlockSpec(memory_space=pl.ANY)] * 2,
        out_specs=(pl.BlockSpec(memory_space=pl.ANY), pl.BlockSpec(memory_space=pl.ANY)),
        scratch_shapes=[
            pltpu.SemaphoreType.DMA((n_sends,)),
            pltpu.SemaphoreType.DMA((4 * ns,)),
            pltpu.SemaphoreType.DMA((ns - 1,)),
            pltpu.SemaphoreType.DMA((ns,)),
            pltpu.SemaphoreType.DMA((2,)),
        ],
        compiler_params=pltpu.CompilerParams(collective_id=1, has_side_effects=True),
    )(rotated, outgoing)


def reduce_scores(partial, ns, nl):
    w = partial.shape[0] // ns
    part = partial.reshape(ns, 1, w)
    out = pl.pallas_call(
        functools.partial(reduce_kernel, ns, nl),
        out_shape=jax.ShapeDtypeStruct((1, w), jnp.float32),
        in_specs=[pl.BlockSpec(memory_space=pltpu.VMEM)],
        out_specs=pl.BlockSpec(memory_space=pltpu.VMEM),
        scratch_shapes=[
            pltpu.VMEM((ns, 1, w), jnp.float32),
            pltpu.VMEM((1, w), jnp.float32),
            pltpu.VMEM((nl, 1, w), jnp.float32),
            pltpu.SemaphoreType.DMA((ns,)),
            pltpu.SemaphoreType.DMA((ns,)),
            pltpu.SemaphoreType.DMA((nl,)),
            pltpu.SemaphoreType.DMA((nl,)),
        ],
        compiler_params=pltpu.CompilerParams(collective_id=0, has_side_effects=True),
    )(part)
    return out.reshape(w)


def body(ns, nl, train_inputs, out_grads, query_blocks, basis_in, basis_out, block_of):
    acts = train_inputs[0]
    grads = out_grads[0]
    query = query_blocks[0]
    owners = block_of[0]
    count = acts.shape[0]
    rotated = turn_rows(acts, basis_in[0])
    width = grads.shape[1] // owners.shape[0]
    outgoing = jnp.stack([lax.dynamic_slice_in_dim(grads, owners[k] * width, width, axis=1) for k in range(owners.shape[0])])
    gathered, arrived = exchange(rotated, outgoing, ns)
    arrived = arrived.reshape(ns * count, width)
    rb = basis_out.shape[-1]
    turned = jnp.concatenate(
        [jnp.dot(arrived[:, e * rb:(e + 1) * rb], basis_out[0, e], preferred_element_type=jnp.float32) for e in range(basis_out.shape[1])],
        axis=1).astype(jnp.bfloat16)
    partial_scores = jnp.sum(
        lax.dot_general(
            gathered.reshape(ns * count, -1),
            query,
            (((1,), (1,)), ((), ())),
            preferred_element_type=jnp.float32,
        )
        * turned.astype(jnp.float32),
        axis=1,
    )
    return reduce_scores(partial_scores, ns, nl)


def solution(mesh):
    ns, nl = mesh.shape["seq"], mesh.shape["layer"]
    placed = (
        P("layer", "seq", None),
        P("layer", "seq", None),
        P("layer", "seq", None),
        P("layer", None, None, None),
        P("layer", "seq", None, None),
        P("layer", None),
    )
    return jax.shard_map(functools.partial(body, ns, nl), mesh=mesh, in_specs=placed, out_specs=P("seq"), check_vma=False)
```

```python
import functools

import jax
import jax.numpy as jnp
from jax import lax
from jax.experimental import pallas as pl
from jax.experimental.pallas import tpu as pltpu
from jax.sharding import PartitionSpec as P

MESH = pl.DeviceIdType.MESH


def turn_rows(rows, basis):
    count = rows.shape[0]
    groups = rows.reshape(count, basis.shape[0], basis.shape[1])
    turned = jnp.einsum("tnr,nrs->tns", groups, basis, preferred_element_type=jnp.float32)
    return turned.reshape(count, -1).astype(jnp.bfloat16)


def reduce_kernel(ns, nl, part_ref, out_ref, slots1, mine, slots2, ssem1, rsem1, ssem2, rsem2):
    ms = lax.axis_index("seq")
    ml = lax.axis_index("layer")
    barrier = pltpu.get_barrier_semaphore()
    for d in range(1, ns):
        pl.semaphore_signal(barrier, inc=1, device_id=(lax.rem(ms + d, ns), ml), device_id_type=MESH)
    for d in range(1, nl):
        pl.semaphore_signal(barrier, inc=1, device_id=(ms, lax.rem(ml + d, nl)), device_id_type=MESH)
    pl.semaphore_wait(barrier, (ns - 1) + (nl - 1))

    sends = []
    for d in range(1, ns):
        j = lax.rem(ms + d, ns)
        c = pltpu.make_async_remote_copy(
            src_ref=part_ref.at[j], dst_ref=slots1.at[ms], send_sem=ssem1.at[j], recv_sem=rsem1.at[ms],
            device_id=(j, ml), device_id_type=MESH)
        c.start()
        sends.append(c)
    slots1[ms] = part_ref[ms]
    for d in range(1, ns):
        i = lax.rem(ms + ns - d, ns)
        pltpu.make_async_remote_copy(
            src_ref=part_ref.at[i], dst_ref=slots1.at[i], send_sem=ssem1.at[i], recv_sem=rsem1.at[i],
            device_id=(i, ml), device_id_type=MESH).wait_recv()
    for c in sends:
        c.wait_send()
    acc = slots1[0]
    for i in range(1, ns):
        acc = acc + slots1[i]
    mine[...] = acc

    sends = []
    for d in range(1, nl):
        j = lax.rem(ml + d, nl)
        c = pltpu.make_async_remote_copy(
            src_ref=mine, dst_ref=slots2.at[ml], send_sem=ssem2.at[j], recv_sem=rsem2.at[ml],
            device_id=(ms, j), device_id_type=MESH)
        c.start()
        sends.append(c)
    slots2[ml] = acc
    for d in range(1, nl):
        i = lax.rem(ml + nl - d, nl)
        pltpu.make_async_remote_copy(
            src_ref=mine, dst_ref=slots2.at[i], send_sem=ssem2.at[i], recv_sem=rsem2.at[i],
            device_id=(ms, i), device_id_type=MESH).wait_recv()
    for c in sends:
        c.wait_send()
    tot = slots2[0]
    for i in range(1, nl):
        tot = tot + slots2[i]
    out_ref[...] = tot


def comm_kernel(nx, nz, r1, x_ref, g_ref, xo_ref, go_ref, ssem, rsem, gssem, grsem, lsem):
    ns = nx * nz
    t = x_ref.shape[0]
    s = lax.axis_index("seq")
    lay = lax.axis_index("layer")
    zl = s // nx
    xx = lax.rem(s, nx)
    ha, hb = r1 // 2, (t - r1) // 2
    halves = ((pl.ds(0, ha), pl.ds(ha, ha)), (pl.ds(r1, hb), pl.ds(r1 + hb, hb)))
    whole = (pl.ds(0, r1), pl.ds(r1, t - r1))

    def at(dz, dx):
        return lax.rem(zl + dz + nz, nz) * nx + lax.rem(xx + dx + nx, nx)

    barrier = pltpu.get_barrier_semaphore()
    for d in range(1, ns):
        pl.semaphore_signal(barrier, inc=1, device_id=(lax.rem(s + d, ns), lay), device_id_type=MESH)
    pl.semaphore_wait(barrier, ns - 1)

    own_x = pltpu.make_async_copy(x_ref, xo_ref.at[s], lsem.at[0])
    own_g = pltpu.make_async_copy(g_ref.at[s], go_ref.at[s], lsem.at[1])
    own_x.start()
    own_g.start()

    sends = []

    def rows(part, half):
        return whole[part] if half is None else halves[part][half]

    def sem(slot, part, half):
        return rsem.at[slot * 4 + part * 2 + (0 if half is None else half)]

    def send(dz, dx, part, half, to):
        slot = at(dz, dx)
        rr = rows(part, half)
        src = x_ref.at[rr] if (dz, dx) == (0, 0) else xo_ref.at[slot, rr]
        c = pltpu.make_async_remote_copy(
            src_ref=src, dst_ref=xo_ref.at[slot, rr], send_sem=ssem.at[len(sends)],
            recv_sem=sem(slot, part, half), device_id=(to, lay), device_id_type=MESH)
        c.start()
        sends.append(c)

    def recv(dz, dx, part, half):
        slot = at(dz, dx)
        rr = rows(part, half)
        pltpu.make_async_remote_copy(
            src_ref=x_ref.at[rr], dst_ref=xo_ref.at[slot, rr], send_sem=ssem.at[0],
            recv_sem=sem(slot, part, half), device_id=(slot, lay), device_id_type=MESH).wait_recv()

    right, left = at(0, 1), at(0, -1)
    zpeers = [at(dz, 0) for dz in range(1, nz)]
    for h in range(2 if r1 else 0):
        send(0, 0, 0, h, right)
        send(0, 0, 0, h, left)
    for zp in zpeers:
        if r1:
            send(0, 0, 0, None, zp)
        send(0, 0, 1, None, zp)
    for h in range(2):
        send(0, 0, 1, h, right)
        send(0, 0, 1, h, left)
    gsends = []
    for d in range(1, ns):
        j = lax.rem(s + d, ns)
        c = pltpu.make_async_remote_copy(
            src_ref=g_ref.at[j], dst_ref=go_ref.at[s], send_sem=gssem.at[d - 1],
            recv_sem=grsem.at[s], device_id=(j, lay), device_id_type=MESH)
        c.start()
        gsends.append(c)
    if r1:
        recv(0, -1, 0, 0)
        send(0, -1, 0, 0, right)
        recv(0, 1, 0, 1)
        send(0, 1, 0, 1, left)
        recv(0, -1, 0, 1)
        recv(0, 1, 0, 0)
        for dx in (-1, 1):
            for zp in zpeers:
                send(0, dx, 0, None, zp)
        recv(0, 2, 0, 0)
        recv(0, 2, 0, 1)
        for zp in zpeers:
            send(0, 2, 0, None, zp)
    for dz in range(1, nz):
        recv(dz, 0, 1, None)
        for h in range(2):
            send(dz, 0, 1, h, right)
            send(dz, 0, 1, h, left)
    for dz in range(nz):
        recv(dz, -1, 1, 0)
        send(dz, -1, 1, 0, right)
        recv(dz, 1, 1, 1)
        send(dz, 1, 1, 1, left)
    for dz in range(1, nz if r1 else 1):
        for dx in range(nx):
            recv(dz, dx, 0, None)
    for dz in range(nz):
        recv(dz, -1, 1, 1)
        recv(dz, 1, 1, 0)
        recv(dz, 2, 1, 0)
        recv(dz, 2, 1, 1)
    for d in range(1, ns):
        i = lax.rem(s + ns - d, ns)
        pltpu.make_async_remote_copy(
            src_ref=g_ref.at[i], dst_ref=go_ref.at[i], send_sem=gssem.at[d - 1],
            recv_sem=grsem.at[i], device_id=(i, lay), device_id_type=MESH).wait_recv()
    for c in sends + gsends:
        c.wait_send()
    own_x.wait()
    own_g.wait()


def exchange(rotated, outgoing, ns):
    nx = 4
    nz = ns // nx
    t, dim = rotated.shape
    w = outgoing.shape[-1]
    r1 = 0
    n_sends = 64
    return pl.pallas_call(
        functools.partial(comm_kernel, nx, nz, r1),
        out_shape=(jax.ShapeDtypeStruct((ns, t, dim), rotated.dtype), jax.ShapeDtypeStruct((ns, t, w), outgoing.dtype)),
        in_specs=[pl.BlockSpec(memory_space=pl.ANY)] * 2,
        out_specs=(pl.BlockSpec(memory_space=pl.ANY), pl.BlockSpec(memory_space=pl.ANY)),
        scratch_shapes=[
            pltpu.SemaphoreType.DMA((n_sends,)),
            pltpu.SemaphoreType.DMA((4 * ns,)),
            pltpu.SemaphoreType.DMA((ns - 1,)),
            pltpu.SemaphoreType.DMA((ns,)),
            pltpu.SemaphoreType.DMA((2,)),
        ],
        compiler_params=pltpu.CompilerParams(collective_id=1, has_side_effects=True),
    )(rotated, outgoing)


def reduce_scores(partial, ns, nl):
    w = partial.shape[0] // ns
    part = partial.reshape(ns, 1, w)
    out = pl.pallas_call(
        functools.partial(reduce_kernel, ns, nl),
        out_shape=jax.ShapeDtypeStruct((1, w), jnp.float32),
        in_specs=[pl.BlockSpec(memory_space=pltpu.VMEM)],
        out_specs=pl.BlockSpec(memory_space=pltpu.VMEM),
        scratch_shapes=[
            pltpu.VMEM((ns, 1, w), jnp.float32),
            pltpu.VMEM((1, w), jnp.float32),
            pltpu.VMEM((nl, 1, w), jnp.float32),
            pltpu.SemaphoreType.DMA((ns,)),
            pltpu.SemaphoreType.DMA((ns,)),
            pltpu.SemaphoreType.DMA((nl,)),
            pltpu.SemaphoreType.DMA((nl,)),
        ],
        compiler_params=pltpu.CompilerParams(collective_id=0, has_side_effects=True),
    )(part)
    return out.reshape(w)


def body(ns, nl, train_inputs, out_grads, query_blocks, basis_in, basis_out, block_of):
    acts = train_inputs[0]
    grads = out_grads[0]
    query = query_blocks[0]
    owners = block_of[0]
    count = acts.shape[0]
    rotated = turn_rows(acts, basis_in[0])
    width = grads.shape[1] // owners.shape[0]
    outgoing = jnp.stack([lax.dynamic_slice_in_dim(grads, owners[k] * width, width, axis=1) for k in range(owners.shape[0])])
    gathered, arrived = exchange(rotated, outgoing, ns)
    arrived = arrived.reshape(ns * count, width)
    rb = basis_out.shape[-1]
    turned = jnp.concatenate(
        [jnp.dot(arrived[:, e * rb:(e + 1) * rb], basis_out[0, e], preferred_element_type=jnp.float32) for e in range(basis_out.shape[1])],
        axis=1).astype(jnp.bfloat16)
    partial_scores = jnp.sum(
        lax.dot_general(
            gathered.reshape(ns * count, -1),
            query,
            (((1,), (1,)), ((), ())),
            preferred_element_type=jnp.float32,
        )
        * turned.astype(jnp.float32),
        axis=1,
    )
    return reduce_scores(partial_scores, ns, nl)


def solution(mesh):
    ns, nl = mesh.shape["seq"], mesh.shape["layer"]
    placed = (
        P("layer", "seq", None),
        P("layer", "seq", None),
        P("layer", "seq", None),
        P("layer", None, None, None),
        P("layer", "seq", None, None),
        P("layer", None),
    )
    return jax.shard_map(functools.partial(body, ns, nl), mesh=mesh, in_specs=placed, out_specs=P("seq"), check_vma=False)
```

```python
import functools

import jax
import jax.numpy as jnp
from jax import lax
from jax.experimental import pallas as pl
from jax.experimental.pallas import tpu as pltpu
from jax.sharding import PartitionSpec as P

MESH = pl.DeviceIdType.MESH


def turn_rows(rows, basis):
    count = rows.shape[0]
    groups = rows.reshape(count, basis.shape[0], basis.shape[1])
    turned = jnp.einsum("tnr,nrs->tns", groups, basis, preferred_element_type=jnp.float32)
    return turned.reshape(count, -1).astype(jnp.bfloat16)


def reduce_kernel(ns, nl, part_ref, out_ref, slots1, mine, slots2, ssem1, rsem1, ssem2, rsem2):
    ms = lax.axis_index("seq")
    ml = lax.axis_index("layer")
    barrier = pltpu.get_barrier_semaphore()
    for d in range(1, ns):
        pl.semaphore_signal(barrier, inc=1, device_id=(lax.rem(ms + d, ns), ml), device_id_type=MESH)
    for d in range(1, nl):
        pl.semaphore_signal(barrier, inc=1, device_id=(ms, lax.rem(ml + d, nl)), device_id_type=MESH)
    pl.semaphore_wait(barrier, (ns - 1) + (nl - 1))

    sends = []
    for d in range(1, ns):
        j = lax.rem(ms + d, ns)
        c = pltpu.make_async_remote_copy(
            src_ref=part_ref.at[j], dst_ref=slots1.at[ms], send_sem=ssem1.at[j], recv_sem=rsem1.at[ms],
            device_id=(j, ml), device_id_type=MESH)
        c.start()
        sends.append(c)
    slots1[ms] = part_ref[ms]
    for d in range(1, ns):
        i = lax.rem(ms + ns - d, ns)
        pltpu.make_async_remote_copy(
            src_ref=part_ref.at[i], dst_ref=slots1.at[i], send_sem=ssem1.at[i], recv_sem=rsem1.at[i],
            device_id=(i, ml), device_id_type=MESH).wait_recv()
    for c in sends:
        c.wait_send()
    acc = slots1[0]
    for i in range(1, ns):
        acc = acc + slots1[i]
    mine[...] = acc

    sends = []
    for d in range(1, nl):
        j = lax.rem(ml + d, nl)
        c = pltpu.make_async_remote_copy(
            src_ref=mine, dst_ref=slots2.at[ml], send_sem=ssem2.at[j], recv_sem=rsem2.at[ml],
            device_id=(ms, j), device_id_type=MESH)
        c.start()
        sends.append(c)
    slots2[ml] = acc
    for d in range(1, nl):
        i = lax.rem(ml + nl - d, nl)
        pltpu.make_async_remote_copy(
            src_ref=mine, dst_ref=slots2.at[i], send_sem=ssem2.at[i], recv_sem=rsem2.at[i],
            device_id=(ms, i), device_id_type=MESH).wait_recv()
    for c in sends:
        c.wait_send()
    tot = slots2[0]
    for i in range(1, nl):
        tot = tot + slots2[i]
    out_ref[...] = tot


def comm_kernel(nx, nz, r1, x_ref, g_ref, xo_ref, go_ref, ssem, rsem, gssem, grsem, lsem):
    ns = nx * nz
    t = x_ref.shape[0]
    s = lax.axis_index("seq")
    lay = lax.axis_index("layer")
    zl = s // nx
    xx = lax.rem(s, nx)
    ha, hb = r1 // 2, (t - r1) // 2
    halves = ((pl.ds(0, ha), pl.ds(ha, ha)), (pl.ds(r1, hb), pl.ds(r1 + hb, hb)))
    whole = (pl.ds(0, r1), pl.ds(r1, t - r1))
    offsets = [e for k in range(1, nz) for e in (k, -k)]

    def on_line(e):
        return jnp.logical_and(zl + e >= 0, zl + e < nz)

    def at(e, dx):
        row = jnp.clip(zl + e, 0, nz - 1)
        return row * nx + lax.rem(xx + dx + nx, nx)

    barrier = pltpu.get_barrier_semaphore()
    for d in range(1, ns):
        pl.semaphore_signal(barrier, inc=1, device_id=(lax.rem(s + d, ns), lay), device_id_type=MESH)
    pl.semaphore_wait(barrier, ns - 1)

    own_x = pltpu.make_async_copy(x_ref, xo_ref.at[s], lsem.at[0])
    own_g = pltpu.make_async_copy(g_ref.at[s], go_ref.at[s], lsem.at[1])
    own_x.start()
    own_g.start()

    sends = []

    def rows(part, half):
        return whole[part] if half is None else halves[part][half]

    def sem(slot, part, half):
        return rsem.at[slot * 4 + part * 2 + (0 if half is None else half)]

    def guarded(cond, fn):
        if cond is None:
            fn()
        else:
            pl.when(cond)(fn)

    def send(e, dx, part, half, to, cond=None):
        slot = at(e, dx)
        rr = rows(part, half)
        src = x_ref.at[rr] if (e, dx) == (0, 0) else xo_ref.at[slot, rr]
        c = pltpu.make_async_remote_copy(
            src_ref=src, dst_ref=xo_ref.at[slot, rr], send_sem=ssem.at[len(sends)],
            recv_sem=sem(slot, part, half), device_id=(to, lay), device_id_type=MESH)
        guarded(cond, c.start)
        sends.append((c, cond))

    def recv(e, dx, part, half, cond=None):
        slot = at(e, dx)
        rr = rows(part, half)
        c = pltpu.make_async_remote_copy(
            src_ref=x_ref.at[rr], dst_ref=xo_ref.at[slot, rr], send_sem=ssem.at[0],
            recv_sem=sem(slot, part, half), device_id=(slot, lay), device_id_type=MESH)
        guarded(cond, c.wait_recv)

    right, left = at(0, 1), at(0, -1)
    for e in offsets:
        send(0, 0, 1, None, at(e, 0), on_line(e))
    for h in range(2):
        send(0, 0, 1, h, right)
        send(0, 0, 1, h, left)
    if r1:
        for h in range(2):
            send(0, 0, 0, h, right)
            send(0, 0, 0, h, left)
        for e in offsets:
            send(0, 0, 0, None, at(e, 0), on_line(e))
    for e in offsets:
        cond = on_line(e)
        recv(e, 0, 1, None, cond)
        for h in range(2):
            send(e, 0, 1, h, right, cond)
            send(e, 0, 1, h, left, cond)
    gsends = []
    for d in range(1, ns):
        j = lax.rem(s + d, ns)
        c = pltpu.make_async_remote_copy(
            src_ref=g_ref.at[j], dst_ref=go_ref.at[s], send_sem=gssem.at[d - 1],
            recv_sem=grsem.at[s], device_id=(j, lay), device_id_type=MESH)
        c.start()
        gsends.append(c)
    if r1:
        recv(0, -1, 0, 0)
        send(0, -1, 0, 0, right)
        recv(0, 1, 0, 1)
        send(0, 1, 0, 1, left)
        recv(0, -1, 0, 1)
        recv(0, 1, 0, 0)
        for e in offsets:
            for dx in (-1, 1):
                send(0, dx, 0, None, at(e, 0), on_line(e))
        recv(0, 2, 0, 0)
        recv(0, 2, 0, 1)
        for e in offsets:
            send(0, 2, 0, None, at(e, 0), on_line(e))
    for e, cond in [(0, None)] + [(e, on_line(e)) for e in offsets]:
        recv(e, -1, 1, 0, cond)
        send(e, -1, 1, 0, right, cond)
        recv(e, 1, 1, 1, cond)
        send(e, 1, 1, 1, left, cond)
    if r1:
        for e in offsets:
            for dx in range(nx):
                recv(e, dx, 0, None, on_line(e))
    for e, cond in [(0, None)] + [(e, on_line(e)) for e in offsets]:
        recv(e, -1, 1, 1, cond)
        recv(e, 1, 1, 0, cond)
        recv(e, 2, 1, 0, cond)
        recv(e, 2, 1, 1, cond)
    for d in range(1, ns):
        i = lax.rem(s + ns - d, ns)
        pltpu.make_async_remote_copy(
            src_ref=g_ref.at[i], dst_ref=go_ref.at[i], send_sem=gssem.at[d - 1],
            recv_sem=grsem.at[i], device_id=(i, lay), device_id_type=MESH).wait_recv()
    for c, cond in sends:
        guarded(cond, c.wait_send)
    for c in gsends:
        c.wait_send()
    own_x.wait()
    own_g.wait()


def exchange(rotated, outgoing, ns):
    nx = 4
    nz = ns // nx
    t, dim = rotated.shape
    w = outgoing.shape[-1]
    r1 = 0
    n_sends = 128
    return pl.pallas_call(
        functools.partial(comm_kernel, nx, nz, r1),
        out_shape=(jax.ShapeDtypeStruct((ns, t, dim), rotated.dtype), jax.ShapeDtypeStruct((ns, t, w), outgoing.dtype)),
        in_specs=[pl.BlockSpec(memory_space=pl.ANY)] * 2,
        out_specs=(pl.BlockSpec(memory_space=pl.ANY), pl.BlockSpec(memory_space=pl.ANY)),
        scratch_shapes=[
            pltpu.SemaphoreType.DMA((n_sends,)),
            pltpu.SemaphoreType.DMA((4 * ns,)),
            pltpu.SemaphoreType.DMA((ns - 1,)),
            pltpu.SemaphoreType.DMA((ns,)),
            pltpu.SemaphoreType.DMA((2,)),
        ],
        compiler_params=pltpu.CompilerParams(collective_id=1, has_side_effects=True),
    )(rotated, outgoing)


def pick_kernel(owners_ref, g_ref, o_ref):
    o_ref[0] = g_ref[...]


def pick_blocks(grads, owners):
    count, total = grads.shape
    nblk = owners.shape[0]
    width = total // nblk
    return pl.pallas_call(
        pick_kernel,
        out_shape=jax.ShapeDtypeStruct((nblk, count, width), grads.dtype),
        grid_spec=pltpu.PrefetchScalarGridSpec(
            num_scalar_prefetch=1,
            grid=(nblk,),
            in_specs=[pl.BlockSpec((count, width), lambda k, own: (0, own[k]))],
            out_specs=pl.BlockSpec((1, count, width), lambda k, own: (k, 0, 0)),
        ),
    )(owners, grads)


def reduce_scores(partial, ns, nl):
    w = partial.shape[0] // ns
    part = partial.reshape(ns, 1, w)
    out = pl.pallas_call(
        functools.partial(reduce_kernel, ns, nl),
        out_shape=jax.ShapeDtypeStruct((1, w), jnp.float32),
        in_specs=[pl.BlockSpec(memory_space=pltpu.VMEM)],
        out_specs=pl.BlockSpec(memory_space=pltpu.VMEM),
        scratch_shapes=[
            pltpu.VMEM((ns, 1, w), jnp.float32),
            pltpu.VMEM((1, w), jnp.float32),
            pltpu.VMEM((nl, 1, w), jnp.float32),
            pltpu.SemaphoreType.DMA((ns,)),
            pltpu.SemaphoreType.DMA((ns,)),
            pltpu.SemaphoreType.DMA((nl,)),
            pltpu.SemaphoreType.DMA((nl,)),
        ],
        compiler_params=pltpu.CompilerParams(collective_id=0, has_side_effects=True),
    )(part)
    return out.reshape(w)


def body(ns, nl, train_inputs, out_grads, query_blocks, basis_in, basis_out, block_of):
    acts = train_inputs[0]
    grads = out_grads[0]
    query = query_blocks[0]
    owners = block_of[0]
    count = acts.shape[0]
    rotated = turn_rows(acts, basis_in[0])
    width = grads.shape[1] // owners.shape[0]
    outgoing = pick_blocks(grads, owners)
    gathered, arrived = exchange(rotated, outgoing, ns)
    arrived = arrived.reshape(ns * count, width)
    rb = basis_out.shape[-1]
    turned = jnp.concatenate(
        [jnp.dot(arrived[:, e * rb:(e + 1) * rb], basis_out[0, e], preferred_element_type=jnp.float32) for e in range(basis_out.shape[1])],
        axis=1).astype(jnp.bfloat16)
    partial_scores = jnp.sum(
        lax.dot_general(
            gathered.reshape(ns * count, -1),
            query,
            (((1,), (1,)), ((), ())),
            preferred_element_type=jnp.float32,
        )
        * turned.astype(jnp.float32),
        axis=1,
    )
    return reduce_scores(partial_scores, ns, nl)


def solution(mesh):
    ns, nl = mesh.shape["seq"], mesh.shape["layer"]
    placed = (
        P("layer", "seq", None),
        P("layer", "seq", None),
        P("layer", "seq", None),
        P("layer", None, None, None),
        P("layer", "seq", None, None),
        P("layer", None),
    )
    return jax.shard_map(functools.partial(body, ns, nl), mesh=mesh, in_specs=placed, out_specs=P("seq"), check_vma=False)
```

```python
import functools

import jax
import jax.numpy as jnp
from jax import lax
from jax.experimental import pallas as pl
from jax.experimental.pallas import tpu as pltpu
from jax.sharding import PartitionSpec as P

MESH = pl.DeviceIdType.MESH


def turn_rows(rows, basis):
    count = rows.shape[0]
    groups = rows.reshape(count, basis.shape[0], basis.shape[1])
    turned = jnp.einsum("tnr,nrs->tns", groups, basis, preferred_element_type=jnp.float32)
    return turned.reshape(count, -1).astype(jnp.bfloat16)


def reduce_kernel(ns, nl, part_ref, out_ref, slots1, mine, slots2, ssem1, rsem1, ssem2, rsem2):
    ms = lax.axis_index("seq")
    ml = lax.axis_index("layer")
    barrier = pltpu.get_barrier_semaphore()
    for d in range(1, ns):
        pl.semaphore_signal(barrier, inc=1, device_id=(lax.rem(ms + d, ns), ml), device_id_type=MESH)
    for d in range(1, nl):
        pl.semaphore_signal(barrier, inc=1, device_id=(ms, lax.rem(ml + d, nl)), device_id_type=MESH)
    pl.semaphore_wait(barrier, (ns - 1) + (nl - 1))

    sends = []
    for d in range(1, ns):
        j = lax.rem(ms + d, ns)
        c = pltpu.make_async_remote_copy(
            src_ref=part_ref.at[j], dst_ref=slots1.at[ms], send_sem=ssem1.at[j], recv_sem=rsem1.at[ms],
            device_id=(j, ml), device_id_type=MESH)
        c.start()
        sends.append(c)
    slots1[ms] = part_ref[ms]
    for d in range(1, ns):
        i = lax.rem(ms + ns - d, ns)
        pltpu.make_async_remote_copy(
            src_ref=part_ref.at[i], dst_ref=slots1.at[i], send_sem=ssem1.at[i], recv_sem=rsem1.at[i],
            device_id=(i, ml), device_id_type=MESH).wait_recv()
    for c in sends:
        c.wait_send()
    acc = slots1[0]
    for i in range(1, ns):
        acc = acc + slots1[i]
    mine[...] = acc

    sends = []
    for d in range(1, nl):
        j = lax.rem(ml + d, nl)
        c = pltpu.make_async_remote_copy(
            src_ref=mine, dst_ref=slots2.at[ml], send_sem=ssem2.at[j], recv_sem=rsem2.at[ml],
            device_id=(ms, j), device_id_type=MESH)
        c.start()
        sends.append(c)
    slots2[ml] = acc
    for d in range(1, nl):
        i = lax.rem(ml + nl - d, nl)
        pltpu.make_async_remote_copy(
            src_ref=mine, dst_ref=slots2.at[i], send_sem=ssem2.at[i], recv_sem=rsem2.at[i],
            device_id=(ms, i), device_id_type=MESH).wait_recv()
    for c in sends:
        c.wait_send()
    tot = slots2[0]
    for i in range(1, nl):
        tot = tot + slots2[i]
    out_ref[...] = tot


def comm_kernel(nx, nz, r1, x_ref, g_ref, xo_ref, go_ref, ssem, rsem, gssem, grsem, lsem):
    ns = nx * nz
    t = x_ref.shape[0]
    s = lax.axis_index("seq")
    lay = lax.axis_index("layer")
    zl = s // nx
    xx = lax.rem(s, nx)
    ha, hb = r1 // 2, (t - r1) // 2
    halves = ((pl.ds(0, ha), pl.ds(ha, ha)), (pl.ds(r1, hb), pl.ds(r1 + hb, hb)))
    whole = (pl.ds(0, r1), pl.ds(r1, t - r1))
    offsets = [e for k in range(1, nz) for e in (k, -k)]

    def on_line(e):
        return jnp.logical_and(zl + e >= 0, zl + e < nz)

    def at(e, dx):
        row = jnp.clip(zl + e, 0, nz - 1)
        return row * nx + lax.rem(xx + dx + nx, nx)

    barrier = pltpu.get_barrier_semaphore()
    for d in range(1, ns):
        pl.semaphore_signal(barrier, inc=1, device_id=(lax.rem(s + d, ns), lay), device_id_type=MESH)
    pl.semaphore_wait(barrier, ns - 1)

    own_x = pltpu.make_async_copy(x_ref, xo_ref.at[s], lsem.at[0])
    own_g = pltpu.make_async_copy(g_ref.at[s], go_ref.at[s], lsem.at[1])
    own_x.start()
    own_g.start()

    sends = []

    def rows(part, half):
        return whole[part] if half is None else halves[part][half]

    def sem(slot, part, half):
        return rsem.at[slot * 4 + part * 2 + (0 if half is None else half)]

    def guarded(cond, fn):
        if cond is None:
            fn()
        else:
            pl.when(cond)(fn)

    def send(e, dx, part, half, to, cond=None):
        slot = at(e, dx)
        rr = rows(part, half)
        src = x_ref.at[rr] if (e, dx) == (0, 0) else xo_ref.at[slot, rr]
        c = pltpu.make_async_remote_copy(
            src_ref=src, dst_ref=xo_ref.at[slot, rr], send_sem=ssem.at[len(sends)],
            recv_sem=sem(slot, part, half), device_id=(to, lay), device_id_type=MESH)
        guarded(cond, c.start)
        sends.append((c, cond))

    def recv(e, dx, part, half, cond=None):
        slot = at(e, dx)
        rr = rows(part, half)
        c = pltpu.make_async_remote_copy(
            src_ref=x_ref.at[rr], dst_ref=xo_ref.at[slot, rr], send_sem=ssem.at[0],
            recv_sem=sem(slot, part, half), device_id=(slot, lay), device_id_type=MESH)
        guarded(cond, c.wait_recv)

    right, left = at(0, 1), at(0, -1)
    for e in offsets:
        send(0, 0, 1, None, at(e, 0), on_line(e))
    for h in range(2):
        send(0, 0, 1, h, right)
        send(0, 0, 1, h, left)
    if r1:
        for h in range(2):
            send(0, 0, 0, h, right)
            send(0, 0, 0, h, left)
        for e in offsets:
            send(0, 0, 0, None, at(e, 0), on_line(e))
    gsends = []
    for d in range(1, ns):
        j = lax.rem(s + d, ns)
        c = pltpu.make_async_remote_copy(
            src_ref=g_ref.at[j], dst_ref=go_ref.at[s], send_sem=gssem.at[d - 1],
            recv_sem=grsem.at[s], device_id=(j, lay), device_id_type=MESH)
        c.start()
        gsends.append(c)
    for e in offsets:
        cond = on_line(e)
        recv(e, 0, 1, None, cond)
        for h in range(2):
            send(e, 0, 1, h, right, cond)
            send(e, 0, 1, h, left, cond)
    if r1:
        recv(0, -1, 0, 0)
        send(0, -1, 0, 0, right)
        recv(0, 1, 0, 1)
        send(0, 1, 0, 1, left)
        recv(0, -1, 0, 1)
        recv(0, 1, 0, 0)
        for e in offsets:
            for dx in (-1, 1):
                send(0, dx, 0, None, at(e, 0), on_line(e))
        recv(0, 2, 0, 0)
        recv(0, 2, 0, 1)
        for e in offsets:
            send(0, 2, 0, None, at(e, 0), on_line(e))
    for e, cond in [(0, None)] + [(e, on_line(e)) for e in offsets]:
        recv(e, -1, 1, 0, cond)
        send(e, -1, 1, 0, right, cond)
        recv(e, 1, 1, 1, cond)
        send(e, 1, 1, 1, left, cond)
    if r1:
        for e in offsets:
            for dx in range(nx):
                recv(e, dx, 0, None, on_line(e))
    for e, cond in [(0, None)] + [(e, on_line(e)) for e in offsets]:
        recv(e, -1, 1, 1, cond)
        recv(e, 1, 1, 0, cond)
        recv(e, 2, 1, 0, cond)
        recv(e, 2, 1, 1, cond)
    for d in range(1, ns):
        i = lax.rem(s + ns - d, ns)
        pltpu.make_async_remote_copy(
            src_ref=g_ref.at[i], dst_ref=go_ref.at[i], send_sem=gssem.at[d - 1],
            recv_sem=grsem.at[i], device_id=(i, lay), device_id_type=MESH).wait_recv()
    for c, cond in sends:
        guarded(cond, c.wait_send)
    for c in gsends:
        c.wait_send()
    own_x.wait()
    own_g.wait()


def exchange(rotated, outgoing, ns):
    nx = 4
    nz = ns // nx
    t, dim = rotated.shape
    w = outgoing.shape[-1]
    r1 = t // 8
    n_sends = 128
    return pl.pallas_call(
        functools.partial(comm_kernel, nx, nz, r1),
        out_shape=(jax.ShapeDtypeStruct((ns, t, dim), rotated.dtype), jax.ShapeDtypeStruct((ns, t, w), outgoing.dtype)),
        in_specs=[pl.BlockSpec(memory_space=pl.ANY)] * 2,
        out_specs=(pl.BlockSpec(memory_space=pl.ANY), pl.BlockSpec(memory_space=pl.ANY)),
        scratch_shapes=[
            pltpu.SemaphoreType.DMA((n_sends,)),
            pltpu.SemaphoreType.DMA((4 * ns,)),
            pltpu.SemaphoreType.DMA((ns - 1,)),
            pltpu.SemaphoreType.DMA((ns,)),
            pltpu.SemaphoreType.DMA((2,)),
        ],
        compiler_params=pltpu.CompilerParams(collective_id=1, has_side_effects=True),
    )(rotated, outgoing)


def pick_kernel(owners_ref, *refs):
    o_ref = refs[-1]
    for i, g_ref in enumerate(refs[:-1]):
        o_ref[i] = g_ref[...]


def pick_blocks(grads, owners, per_step=4):
    count, total = grads.shape
    nblk = owners.shape[0]
    width = total // nblk

    def spec(i):
        return pl.BlockSpec((count, width), lambda k, own: (0, own[k * per_step + i]))

    return pl.pallas_call(
        pick_kernel,
        out_shape=jax.ShapeDtypeStruct((nblk, count, width), grads.dtype),
        grid_spec=pltpu.PrefetchScalarGridSpec(
            num_scalar_prefetch=1,
            grid=(nblk // per_step,),
            in_specs=[spec(i) for i in range(per_step)],
            out_specs=pl.BlockSpec((per_step, count, width), lambda k, own: (k, 0, 0)),
        ),
    )(owners, *([grads] * per_step))


def reduce_scores(partial, ns, nl):
    w = partial.shape[0] // ns
    part = partial.reshape(ns, 1, w)
    out = pl.pallas_call(
        functools.partial(reduce_kernel, ns, nl),
        out_shape=jax.ShapeDtypeStruct((1, w), jnp.float32),
        in_specs=[pl.BlockSpec(memory_space=pltpu.VMEM)],
        out_specs=pl.BlockSpec(memory_space=pltpu.VMEM),
        scratch_shapes=[
            pltpu.VMEM((ns, 1, w), jnp.float32),
            pltpu.VMEM((1, w), jnp.float32),
            pltpu.VMEM((nl, 1, w), jnp.float32),
            pltpu.SemaphoreType.DMA((ns,)),
            pltpu.SemaphoreType.DMA((ns,)),
            pltpu.SemaphoreType.DMA((nl,)),
            pltpu.SemaphoreType.DMA((nl,)),
        ],
        compiler_params=pltpu.CompilerParams(collective_id=0, has_side_effects=True),
    )(part)
    return out.reshape(w)


def body(ns, nl, train_inputs, out_grads, query_blocks, basis_in, basis_out, block_of):
    acts = train_inputs[0]
    grads = out_grads[0]
    query = query_blocks[0]
    owners = block_of[0]
    count = acts.shape[0]
    rotated = turn_rows(acts, basis_in[0])
    width = grads.shape[1] // owners.shape[0]
    outgoing = pick_blocks(grads, owners)
    gathered, arrived = exchange(rotated, outgoing, ns)
    arrived = arrived.reshape(ns * count, width)
    rb = basis_out.shape[-1]
    turned = jnp.concatenate(
        [jnp.dot(arrived[:, e * rb:(e + 1) * rb], basis_out[0, e], preferred_element_type=jnp.float32) for e in range(basis_out.shape[1])],
        axis=1).astype(jnp.bfloat16)
    partial_scores = jnp.sum(
        lax.dot_general(
            gathered.reshape(ns * count, -1),
            query,
            (((1,), (1,)), ((), ())),
            preferred_element_type=jnp.float32,
        )
        * turned.astype(jnp.float32),
        axis=1,
    )
    return reduce_scores(partial_scores, ns, nl)


def solution(mesh):
    ns, nl = mesh.shape["seq"], mesh.shape["layer"]
    placed = (
        P("layer", "seq", None),
        P("layer", "seq", None),
        P("layer", "seq", None),
        P("layer", None, None, None),
        P("layer", "seq", None, None),
        P("layer", None),
    )
    return jax.shard_map(functools.partial(body, ns, nl), mesh=mesh, in_specs=placed, out_specs=P("seq"), check_vma=False)
```

```python
import functools

import jax
import jax.numpy as jnp
from jax import lax
from jax.experimental import pallas as pl
from jax.experimental.pallas import tpu as pltpu
from jax.sharding import PartitionSpec as P

MESH = pl.DeviceIdType.MESH


def turn_rows(rows, basis):
    count = rows.shape[0]
    groups = rows.reshape(count, basis.shape[0], basis.shape[1])
    turned = jnp.einsum("tnr,nrs->tns", groups, basis, preferred_element_type=jnp.float32)
    return turned.reshape(count, -1).astype(jnp.bfloat16)


def reduce_kernel(ns, nl, part_ref, out_ref, slots1, mine, slots2, ssem1, rsem1, ssem2, rsem2):
    ms = lax.axis_index("seq")
    ml = lax.axis_index("layer")
    barrier = pltpu.get_barrier_semaphore()
    for d in range(1, ns):
        pl.semaphore_signal(barrier, inc=1, device_id=(lax.rem(ms + d, ns), ml), device_id_type=MESH)
    for d in range(1, nl):
        pl.semaphore_signal(barrier, inc=1, device_id=(ms, lax.rem(ml + d, nl)), device_id_type=MESH)
    pl.semaphore_wait(barrier, (ns - 1) + (nl - 1))

    sends = []
    for d in range(1, ns):
        j = lax.rem(ms + d, ns)
        c = pltpu.make_async_remote_copy(
            src_ref=part_ref.at[j], dst_ref=slots1.at[ms], send_sem=ssem1.at[j], recv_sem=rsem1.at[ms],
            device_id=(j, ml), device_id_type=MESH)
        c.start()
        sends.append(c)
    slots1[ms] = part_ref[ms]
    for d in range(1, ns):
        i = lax.rem(ms + ns - d, ns)
        pltpu.make_async_remote_copy(
            src_ref=part_ref.at[i], dst_ref=slots1.at[i], send_sem=ssem1.at[i], recv_sem=rsem1.at[i],
            device_id=(i, ml), device_id_type=MESH).wait_recv()
    for c in sends:
        c.wait_send()
    acc = slots1[0]
    for i in range(1, ns):
        acc = acc + slots1[i]
    mine[...] = acc

    sends = []
    for d in range(1, nl):
        j = lax.rem(ml + d, nl)
        c = pltpu.make_async_remote_copy(
            src_ref=mine, dst_ref=slots2.at[ml], send_sem=ssem2.at[j], recv_sem=rsem2.at[ml],
            device_id=(ms, j), device_id_type=MESH)
        c.start()
        sends.append(c)
    slots2[ml] = acc
    for d in range(1, nl):
        i = lax.rem(ml + nl - d, nl)
        pltpu.make_async_remote_copy(
            src_ref=mine, dst_ref=slots2.at[i], send_sem=ssem2.at[i], recv_sem=rsem2.at[i],
            device_id=(ms, i), device_id_type=MESH).wait_recv()
    for c in sends:
        c.wait_send()
    tot = slots2[0]
    for i in range(1, nl):
        tot = tot + slots2[i]
    out_ref[...] = tot


def comm_kernel(nx, nz, r1, x_ref, g_ref, xo_ref, go_ref, ssem, rsem, gssem, grsem, lsem):
    ns = nx * nz
    t = x_ref.shape[0]
    s = lax.axis_index("seq")
    lay = lax.axis_index("layer")
    zl = s // nx
    xx = lax.rem(s, nx)
    ha, hb = r1 // 2, (t - r1) // 2
    halves = ((pl.ds(0, ha), pl.ds(ha, ha)), (pl.ds(r1, hb), pl.ds(r1 + hb, hb)))
    whole = (pl.ds(0, r1), pl.ds(r1, t - r1))
    offsets = [e for k in range(1, nz) for e in (k, -k)]

    def on_line(e):
        return jnp.logical_and(zl + e >= 0, zl + e < nz)

    def at(e, dx):
        row = jnp.clip(zl + e, 0, nz - 1)
        return row * nx + lax.rem(xx + dx + nx, nx)

    barrier = pltpu.get_barrier_semaphore()
    for d in range(1, ns):
        pl.semaphore_signal(barrier, inc=1, device_id=(lax.rem(s + d, ns), lay), device_id_type=MESH)
    pl.semaphore_wait(barrier, ns - 1)

    own_x = pltpu.make_async_copy(x_ref, xo_ref.at[s], lsem.at[0])
    own_g = pltpu.make_async_copy(g_ref.at[s], go_ref.at[s], lsem.at[1])
    own_x.start()
    own_g.start()

    sends = []

    def rows(part, half):
        return whole[part] if half is None else halves[part][half]

    def sem(slot, part, half):
        return rsem.at[slot * 4 + part * 2 + (0 if half is None else half)]

    def guarded(cond, fn):
        if cond is None:
            fn()
        else:
            pl.when(cond)(fn)

    def send(e, dx, part, half, to, cond=None):
        slot = at(e, dx)
        rr = rows(part, half)
        src = x_ref.at[rr] if (e, dx) == (0, 0) else xo_ref.at[slot, rr]
        c = pltpu.make_async_remote_copy(
            src_ref=src, dst_ref=xo_ref.at[slot, rr], send_sem=ssem.at[len(sends)],
            recv_sem=sem(slot, part, half), device_id=(to, lay), device_id_type=MESH)
        guarded(cond, c.start)
        sends.append((c, cond))

    def recv(e, dx, part, half, cond=None):
        slot = at(e, dx)
        rr = rows(part, half)
        c = pltpu.make_async_remote_copy(
            src_ref=x_ref.at[rr], dst_ref=xo_ref.at[slot, rr], send_sem=ssem.at[0],
            recv_sem=sem(slot, part, half), device_id=(slot, lay), device_id_type=MESH)
        guarded(cond, c.wait_recv)

    right, left = at(0, 1), at(0, -1)
    for e in offsets:
        send(0, 0, 1, None, at(e, 0), on_line(e))
    for h in range(2):
        send(0, 0, 1, h, right)
        send(0, 0, 1, h, left)
    if r1:
        for h in range(2):
            send(0, 0, 0, h, right)
            send(0, 0, 0, h, left)
        for e in offsets:
            send(0, 0, 0, None, at(e, 0), on_line(e))
    for e in offsets:
        cond = on_line(e)
        recv(e, 0, 1, None, cond)
        for h in range(2):
            send(e, 0, 1, h, right, cond)
            send(e, 0, 1, h, left, cond)
    if r1:
        recv(0, -1, 0, 0)
        send(0, -1, 0, 0, right)
        recv(0, 1, 0, 1)
        send(0, 1, 0, 1, left)
        recv(0, -1, 0, 1)
        recv(0, 1, 0, 0)
        for e in offsets:
            for dx in (-1, 1):
                send(0, dx, 0, None, at(e, 0), on_line(e))
        recv(0, 2, 0, 0)
        recv(0, 2, 0, 1)
        for e in offsets:
            send(0, 2, 0, None, at(e, 0), on_line(e))
    for e, cond in [(0, None)] + [(e, on_line(e)) for e in offsets]:
        recv(e, -1, 1, 0, cond)
        send(e, -1, 1, 0, right, cond)
        recv(e, 1, 1, 1, cond)
        send(e, 1, 1, 1, left, cond)
    gsends = []
    for d in range(1, ns):
        j = lax.rem(s + d, ns)
        c = pltpu.make_async_remote_copy(
            src_ref=g_ref.at[j], dst_ref=go_ref.at[s], send_sem=gssem.at[d - 1],
            recv_sem=grsem.at[s], device_id=(j, lay), device_id_type=MESH)
        c.start()
        gsends.append(c)
    if r1:
        for e in offsets:
            for dx in range(nx):
                recv(e, dx, 0, None, on_line(e))
    for e, cond in [(0, None)] + [(e, on_line(e)) for e in offsets]:
        recv(e, -1, 1, 1, cond)
        recv(e, 1, 1, 0, cond)
        recv(e, 2, 1, 0, cond)
        recv(e, 2, 1, 1, cond)
    for d in range(1, ns):
        i = lax.rem(s + ns - d, ns)
        pltpu.make_async_remote_copy(
            src_ref=g_ref.at[i], dst_ref=go_ref.at[i], send_sem=gssem.at[d - 1],
            recv_sem=grsem.at[i], device_id=(i, lay), device_id_type=MESH).wait_recv()
    for c, cond in sends:
        guarded(cond, c.wait_send)
    for c in gsends:
        c.wait_send()
    own_x.wait()
    own_g.wait()


def exchange(rotated, outgoing, ns):
    nx = 4
    nz = ns // nx
    t, dim = rotated.shape
    w = outgoing.shape[-1]
    r1 = t // 8
    n_sends = 128
    return pl.pallas_call(
        functools.partial(comm_kernel, nx, nz, r1),
        out_shape=(jax.ShapeDtypeStruct((ns, t, dim), rotated.dtype), jax.ShapeDtypeStruct((ns, t, w), outgoing.dtype)),
        in_specs=[pl.BlockSpec(memory_space=pl.ANY)] * 2,
        out_specs=(pl.BlockSpec(memory_space=pl.ANY), pl.BlockSpec(memory_space=pl.ANY)),
        scratch_shapes=[
            pltpu.SemaphoreType.DMA((n_sends,)),
            pltpu.SemaphoreType.DMA((4 * ns,)),
            pltpu.SemaphoreType.DMA((ns - 1,)),
            pltpu.SemaphoreType.DMA((ns,)),
            pltpu.SemaphoreType.DMA((2,)),
        ],
        compiler_params=pltpu.CompilerParams(collective_id=1, has_side_effects=True),
    )(rotated, outgoing)


def pick_kernel(owners_ref, *refs):
    o_ref = refs[-1]
    for i, g_ref in enumerate(refs[:-1]):
        o_ref[i] = g_ref[...]


def pick_blocks(grads, owners, per_step=4):
    count, total = grads.shape
    nblk = owners.shape[0]
    width = total // nblk

    def spec(i):
        return pl.BlockSpec((count, width), lambda k, own: (0, own[k * per_step + i]))

    return pl.pallas_call(
        pick_kernel,
        out_shape=jax.ShapeDtypeStruct((nblk, count, width), grads.dtype),
        grid_spec=pltpu.PrefetchScalarGridSpec(
            num_scalar_prefetch=1,
            grid=(nblk // per_step,),
            in_specs=[spec(i) for i in range(per_step)],
            out_specs=pl.BlockSpec((per_step, count, width), lambda k, own: (k, 0, 0)),
        ),
    )(owners, *([grads] * per_step))


def reduce_scores(partial, ns, nl):
    w = partial.shape[0] // ns
    part = partial.reshape(ns, 1, w)
    out = pl.pallas_call(
        functools.partial(reduce_kernel, ns, nl),
        out_shape=jax.ShapeDtypeStruct((1, w), jnp.float32),
        in_specs=[pl.BlockSpec(memory_space=pltpu.VMEM)],
        out_specs=pl.BlockSpec(memory_space=pltpu.VMEM),
        scratch_shapes=[
            pltpu.VMEM((ns, 1, w), jnp.float32),
            pltpu.VMEM((1, w), jnp.float32),
            pltpu.VMEM((nl, 1, w), jnp.float32),
            pltpu.SemaphoreType.DMA((ns,)),
            pltpu.SemaphoreType.DMA((ns,)),
            pltpu.SemaphoreType.DMA((nl,)),
            pltpu.SemaphoreType.DMA((nl,)),
        ],
        compiler_params=pltpu.CompilerParams(collective_id=0, has_side_effects=True),
    )(part)
    return out.reshape(w)


def body(ns, nl, train_inputs, out_grads, query_blocks, basis_in, basis_out, block_of):
    acts = train_inputs[0]
    grads = out_grads[0]
    query = query_blocks[0]
    owners = block_of[0]
    count = acts.shape[0]
    rotated = turn_rows(acts, basis_in[0])
    width = grads.shape[1] // owners.shape[0]
    outgoing = pick_blocks(grads, owners)
    gathered, arrived = exchange(rotated, outgoing, ns)
    arrived = arrived.reshape(ns * count, width)
    rb = basis_out.shape[-1]
    turned = jnp.concatenate(
        [jnp.dot(arrived[:, e * rb:(e + 1) * rb], basis_out[0, e], preferred_element_type=jnp.float32) for e in range(basis_out.shape[1])],
        axis=1).astype(jnp.bfloat16)
    partial_scores = jnp.sum(
        lax.dot_general(
            gathered.reshape(ns * count, -1),
            query,
            (((1,), (1,)), ((), ())),
            preferred_element_type=jnp.float32,
        )
        * turned.astype(jnp.float32),
        axis=1,
    )
    return reduce_scores(partial_scores, ns, nl)


def solution(mesh):
    ns, nl = mesh.shape["seq"], mesh.shape["layer"]
    placed = (
        P("layer", "seq", None),
        P("layer", "seq", None),
        P("layer", "seq", None),
        P("layer", None, None, None),
        P("layer", "seq", None, None),
        P("layer", None),
    )
    return jax.shard_map(functools.partial(body, ns, nl), mesh=mesh, in_specs=placed, out_specs=P("seq"), check_vma=False)
```

```python
import functools

import jax
import jax.numpy as jnp
from jax import lax
from jax.experimental import pallas as pl
from jax.experimental.pallas import tpu as pltpu
from jax.sharding import PartitionSpec as P

MESH = pl.DeviceIdType.MESH


def turn_rows(rows, basis):
    count = rows.shape[0]
    groups = rows.reshape(count, basis.shape[0], basis.shape[1])
    turned = jnp.einsum("tnr,nrs->tns", groups, basis, preferred_element_type=jnp.float32)
    return turned.reshape(count, -1).astype(jnp.bfloat16)


def reduce_kernel(ns, nl, part_ref, out_ref, slots1, mine, slots2, ssem1, rsem1, ssem2, rsem2):
    ms = lax.axis_index("seq")
    ml = lax.axis_index("layer")
    barrier = pltpu.get_barrier_semaphore()
    for d in range(1, ns):
        pl.semaphore_signal(barrier, inc=1, device_id=(lax.rem(ms + d, ns), ml), device_id_type=MESH)
    for d in range(1, nl):
        pl.semaphore_signal(barrier, inc=1, device_id=(ms, lax.rem(ml + d, nl)), device_id_type=MESH)
    pl.semaphore_wait(barrier, (ns - 1) + (nl - 1))

    sends = []
    for d in range(1, ns):
        j = lax.rem(ms + d, ns)
        c = pltpu.make_async_remote_copy(
            src_ref=part_ref.at[j], dst_ref=slots1.at[ms], send_sem=ssem1.at[j], recv_sem=rsem1.at[ms],
            device_id=(j, ml), device_id_type=MESH)
        c.start()
        sends.append(c)
    slots1[ms] = part_ref[ms]
    for d in range(1, ns):
        i = lax.rem(ms + ns - d, ns)
        pltpu.make_async_remote_copy(
            src_ref=part_ref.at[i], dst_ref=slots1.at[i], send_sem=ssem1.at[i], recv_sem=rsem1.at[i],
            device_id=(i, ml), device_id_type=MESH).wait_recv()
    for c in sends:
        c.wait_send()
    acc = slots1[0]
    for i in range(1, ns):
        acc = acc + slots1[i]
    mine[...] = acc

    sends = []
    for d in range(1, nl):
        j = lax.rem(ml + d, nl)
        c = pltpu.make_async_remote_copy(
            src_ref=mine, dst_ref=slots2.at[ml], send_sem=ssem2.at[j], recv_sem=rsem2.at[ml],
            device_id=(ms, j), device_id_type=MESH)
        c.start()
        sends.append(c)
    slots2[ml] = acc
    for d in range(1, nl):
        i = lax.rem(ml + nl - d, nl)
        pltpu.make_async_remote_copy(
            src_ref=mine, dst_ref=slots2.at[i], send_sem=ssem2.at[i], recv_sem=rsem2.at[i],
            device_id=(ms, i), device_id_type=MESH).wait_recv()
    for c in sends:
        c.wait_send()
    tot = slots2[0]
    for i in range(1, nl):
        tot = tot + slots2[i]
    out_ref[...] = tot


def comm_kernel(nx, nz, r1, x_ref, g_ref, xo_ref, go_ref, ssem, rsem, gssem, grsem, lsem):
    ns = nx * nz
    t = x_ref.shape[0]
    s = lax.axis_index("seq")
    lay = lax.axis_index("layer")
    zl = s // nx
    xx = lax.rem(s, nx)
    ha, hb = r1 // 2, (t - r1) // 2
    halves = ((pl.ds(0, ha), pl.ds(ha, ha)), (pl.ds(r1, hb), pl.ds(r1 + hb, hb)))
    whole = (pl.ds(0, r1), pl.ds(r1, t - r1))
    offsets = [e for k in range(1, nz) for e in (k, -k)]

    def on_line(e):
        return jnp.logical_and(zl + e >= 0, zl + e < nz)

    def at(e, dx):
        row = jnp.clip(zl + e, 0, nz - 1)
        return row * nx + lax.rem(xx + dx + nx, nx)

    barrier = pltpu.get_barrier_semaphore()
    for d in range(1, ns):
        pl.semaphore_signal(barrier, inc=1, device_id=(lax.rem(s + d, ns), lay), device_id_type=MESH)
    pl.semaphore_wait(barrier, ns - 1)

    own_x = pltpu.make_async_copy(x_ref, xo_ref.at[s], lsem.at[0])
    own_g = pltpu.make_async_copy(g_ref.at[s], go_ref.at[s], lsem.at[1])
    own_x.start()
    own_g.start()

    sends = []

    def rows(part, half):
        return whole[part] if half is None else halves[part][half]

    def sem(slot, part, half):
        return rsem.at[slot * 4 + part * 2 + (0 if half is None else half)]

    def guarded(cond, fn):
        if cond is None:
            fn()
        else:
            pl.when(cond)(fn)

    def send(e, dx, part, half, to, cond=None):
        slot = at(e, dx)
        rr = rows(part, half)
        src = x_ref.at[rr] if (e, dx) == (0, 0) else xo_ref.at[slot, rr]
        c = pltpu.make_async_remote_copy(
            src_ref=src, dst_ref=xo_ref.at[slot, rr], send_sem=ssem.at[len(sends)],
            recv_sem=sem(slot, part, half), device_id=(to, lay), device_id_type=MESH)
        guarded(cond, c.start)
        sends.append((c, cond))

    def recv(e, dx, part, half, cond=None):
        slot = at(e, dx)
        rr = rows(part, half)
        c = pltpu.make_async_remote_copy(
            src_ref=x_ref.at[rr], dst_ref=xo_ref.at[slot, rr], send_sem=ssem.at[0],
            recv_sem=sem(slot, part, half), device_id=(slot, lay), device_id_type=MESH)
        guarded(cond, c.wait_recv)

    right, left = at(0, 1), at(0, -1)
    for e in offsets:
        send(0, 0, 1, None, at(e, 0), on_line(e))
    for h in range(2):
        send(0, 0, 1, h, right)
        send(0, 0, 1, h, left)
    if r1:
        for h in range(2):
            send(0, 0, 0, h, right)
            send(0, 0, 0, h, left)
        for e in offsets:
            send(0, 0, 0, None, at(e, 0), on_line(e))
    for e in offsets:
        cond = on_line(e)
        recv(e, 0, 1, None, cond)
        for h in range(2):
            send(e, 0, 1, h, right, cond)
            send(e, 0, 1, h, left, cond)
    gsends = []
    for e, cond in [(0, None)] + [(e, on_line(e)) for e in offsets]:
        for dx in range(nx):
            if (e, dx) == (0, 0):
                continue
            j = at(e, dx)
            c = pltpu.make_async_remote_copy(
                src_ref=g_ref.at[j], dst_ref=go_ref.at[s], send_sem=gssem.at[len(gsends)],
                recv_sem=grsem.at[s], device_id=(j, lay), device_id_type=MESH)
            guarded(cond, c.start)
            gsends.append((c, cond))
    if r1:
        recv(0, -1, 0, 0)
        send(0, -1, 0, 0, right)
        recv(0, 1, 0, 1)
        send(0, 1, 0, 1, left)
        recv(0, -1, 0, 1)
        recv(0, 1, 0, 0)
        for e in offsets:
            for dx in (-1, 1):
                send(0, dx, 0, None, at(e, 0), on_line(e))
        recv(0, 2, 0, 0)
        recv(0, 2, 0, 1)
        for e in offsets:
            send(0, 2, 0, None, at(e, 0), on_line(e))
    for e, cond in [(0, None)] + [(e, on_line(e)) for e in offsets]:
        recv(e, -1, 1, 0, cond)
        send(e, -1, 1, 0, right, cond)
        recv(e, 1, 1, 1, cond)
        send(e, 1, 1, 1, left, cond)
    if r1:
        for e in offsets:
            for dx in range(nx):
                recv(e, dx, 0, None, on_line(e))
    for e, cond in [(0, None)] + [(e, on_line(e)) for e in offsets]:
        recv(e, -1, 1, 1, cond)
        recv(e, 1, 1, 0, cond)
        recv(e, 2, 1, 0, cond)
        recv(e, 2, 1, 1, cond)
    for d in range(1, ns):
        i = lax.rem(s + ns - d, ns)
        pltpu.make_async_remote_copy(
            src_ref=g_ref.at[i], dst_ref=go_ref.at[i], send_sem=gssem.at[d - 1],
            recv_sem=grsem.at[i], device_id=(i, lay), device_id_type=MESH).wait_recv()
    for c, cond in sends:
        guarded(cond, c.wait_send)
    for c, cond in gsends:
        guarded(cond, c.wait_send)
    own_x.wait()
    own_g.wait()


def exchange(rotated, outgoing, ns):
    nx = 4
    nz = ns // nx
    t, dim = rotated.shape
    w = outgoing.shape[-1]
    r1 = t // 4
    n_sends = 128
    return pl.pallas_call(
        functools.partial(comm_kernel, nx, nz, r1),
        out_shape=(jax.ShapeDtypeStruct((ns, t, dim), rotated.dtype), jax.ShapeDtypeStruct((ns, t, w), outgoing.dtype)),
        in_specs=[pl.BlockSpec(memory_space=pl.ANY)] * 2,
        out_specs=(pl.BlockSpec(memory_space=pl.ANY), pl.BlockSpec(memory_space=pl.ANY)),
        scratch_shapes=[
            pltpu.SemaphoreType.DMA((n_sends,)),
            pltpu.SemaphoreType.DMA((4 * ns,)),
            pltpu.SemaphoreType.DMA((2 * ns,)),
            pltpu.SemaphoreType.DMA((ns,)),
            pltpu.SemaphoreType.DMA((2,)),
        ],
        compiler_params=pltpu.CompilerParams(collective_id=1, has_side_effects=True),
    )(rotated, outgoing)


def pick_kernel(owners_ref, *refs):
    o_ref = refs[-1]
    for i, g_ref in enumerate(refs[:-1]):
        o_ref[i] = g_ref[...]


def pick_blocks(grads, owners, per_step=8):
    count, total = grads.shape
    nblk = owners.shape[0]
    width = total // nblk

    def spec(i):
        return pl.BlockSpec((count, width), lambda k, own: (0, own[k * per_step + i]))

    return pl.pallas_call(
        pick_kernel,
        out_shape=jax.ShapeDtypeStruct((nblk, count, width), grads.dtype),
        grid_spec=pltpu.PrefetchScalarGridSpec(
            num_scalar_prefetch=1,
            grid=(nblk // per_step,),
            in_specs=[spec(i) for i in range(per_step)],
            out_specs=pl.BlockSpec((per_step, count, width), lambda k, own: (k, 0, 0)),
        ),
    )(owners, *([grads] * per_step))


def reduce_scores(partial, ns, nl):
    w = partial.shape[0] // ns
    part = partial.reshape(ns, 1, w)
    out = pl.pallas_call(
        functools.partial(reduce_kernel, ns, nl),
        out_shape=jax.ShapeDtypeStruct((1, w), jnp.float32),
        in_specs=[pl.BlockSpec(memory_space=pltpu.VMEM)],
        out_specs=pl.BlockSpec(memory_space=pltpu.VMEM),
        scratch_shapes=[
            pltpu.VMEM((ns, 1, w), jnp.float32),
            pltpu.VMEM((1, w), jnp.float32),
            pltpu.VMEM((nl, 1, w), jnp.float32),
            pltpu.SemaphoreType.DMA((ns,)),
            pltpu.SemaphoreType.DMA((ns,)),
            pltpu.SemaphoreType.DMA((nl,)),
            pltpu.SemaphoreType.DMA((nl,)),
        ],
        compiler_params=pltpu.CompilerParams(collective_id=0, has_side_effects=True),
    )(part)
    return out.reshape(w)


def body(ns, nl, train_inputs, out_grads, query_blocks, basis_in, basis_out, block_of):
    acts = train_inputs[0]
    grads = out_grads[0]
    query = query_blocks[0]
    owners = block_of[0]
    count = acts.shape[0]
    rotated = turn_rows(acts, basis_in[0])
    width = grads.shape[1] // owners.shape[0]
    outgoing = pick_blocks(grads, owners)
    gathered, arrived = exchange(rotated, outgoing, ns)
    arrived = arrived.reshape(ns * count, width)
    rb = basis_out.shape[-1]
    turned = jnp.concatenate(
        [jnp.dot(arrived[:, e * rb:(e + 1) * rb], basis_out[0, e], preferred_element_type=jnp.float32) for e in range(basis_out.shape[1])],
        axis=1).astype(jnp.bfloat16)
    partial_scores = jnp.sum(
        lax.dot_general(
            gathered.reshape(ns * count, -1),
            query,
            (((1,), (1,)), ((), ())),
            preferred_element_type=jnp.float32,
        )
        * turned.astype(jnp.float32),
        axis=1,
    )
    return reduce_scores(partial_scores, ns, nl)


def solution(mesh):
    ns, nl = mesh.shape["seq"], mesh.shape["layer"]
    placed = (
        P("layer", "seq", None),
        P("layer", "seq", None),
        P("layer", "seq", None),
        P("layer", None, None, None),
        P("layer", "seq", None, None),
        P("layer", None),
    )
    return jax.shard_map(functools.partial(body, ns, nl), mesh=mesh, in_specs=placed, out_specs=P("seq"), check_vma=False)
```
